32 devices in a mesh: chain: 8 (over z, x), pts: 4 (over y, core).
Axes of the slice: x: 2, y: 2, z: 4, core: 2. Of those that a mesh axis runs over, the one named last changes fastest.
Arguments:
- cam_jac: bfloat16 [2048, 12, 512], P(('chain', 'pts')), may hold values from -0.125 to 0.125
- point_jac: bfloat16 [2048, 6, 512], P(('chain', 'pts')), may hold values from -1.5 to 1.5
- residual: float32 [2048, 2, 512], P(('chain', 'pts')), may hold values from -6 to 6
- obs_cam: int32 [2048, 8], P(('chain', 'pts')), may hold values from 0 to 63, all different within a row; in each aligned block of 64 rows (0 to 63, 64 to 127, ...) at most 8 rows name the same one
- damp_exp: int32 [2, 64], replicated, may hold values from -3 to 0
- cam_step: float32 [64, 384], P('chain'), may hold values from -6 to 6
- diag_inverse: bfloat16 [64, 384, 384], P('chain'), may hold values from -0.06 to 0.56
- coupling: bfloat16 [64, 384, 384], P('chain'), may hold values from -33 to 9
Outputs:
- cam_out: float32 [64, 384], P('chain')
- point_out: float32 [2048, 3, 64], P(('chain', 'pts'))
The draws below stay inside these ranges and needn't reach their ends.
Inputs may be any that keep to these rules, and one draw needn't show every extreme that they name: `obs_cam`: in the point blocks of one device no camera block is named by more than 8 of them, and some camera block is named by exactly 8; each row names 8 different camera blocks, and every camera block is named somewhere.
All inputs are finite; a program needn't handle non-finite values.
Results may differ from the reference program's by a relative error of at most 0.0003.
Values sent between devices are 32-bit elements; how exact they have to be, the bound alone decides.
A program may use at most 192 MiB of HBM per device.

```python
import math
import jax
import jax.numpy as jnp
import numpy as np
from jax import lax

BLOCK = 64
TOP = 8
ITERS = 2
PBD = 64
CVEC = 384
NCB = 64
NPB = 2048
OBS_CAM = 256
MOST = 8


def unit_matrix():
    rows_idx = lax.broadcasted_iota(jnp.int32, (CVEC, CVEC), 0)
    cols_idx = lax.broadcasted_iota(jnp.int32, (CVEC, CVEC), 1)
    return (rows_idx == cols_idx).astype(jnp.float32)


def off_noise(noise_key, spread):
    full_shape = (NCB, CVEC, CVEC)
    values = jnp.clip(jax.random.normal(noise_key, full_shape, jnp.float32), -4.0, 4.0)
    return values * (spread / math.sqrt(CVEC))


def draw_diag_inverse(key, part):
    base_key = jax.random.fold_in(key, 17)
    diag_key, noise_key = jax.random.split(base_key)
    panel_scale = math.sqrt(2.0 / NCB)
    diagonal = jax.random.uniform(diag_key, (NCB, CVEC), jnp.float32, 0.9, 1.1)
    unit = unit_matrix()
    return (panel_scale * (off_noise(noise_key, 0.25) * (1.0 - unit) + unit * diagonal[:, :, None])).astype(jnp.bfloat16)


def draw_coupling(key, part):
    base_key = jax.random.fold_in(key, 29)
    diag_key, noise_key = jax.random.split(base_key)
    panel_scale = math.sqrt(NCB / 2.0)
    kept_share = 0.25
    block_gain = kept_share ** (2.0 / NCB)
    centre = math.sqrt((block_gain - 0.0625) / ((1.0 + 0.01 / 3.0 + 0.0625) * (1.0 + 0.01 / 12.0)))
    diagonal = jax.random.uniform(diag_key, (NCB, CVEC), jnp.float32, 0.95 * centre, 1.05 * centre)
    unit = unit_matrix()
    return (-panel_scale * (off_noise(noise_key, 0.25) * (1.0 - unit) + unit * diagonal[:, :, None])).astype(jnp.bfloat16)


def set_ends(array, rng, low, high):
    shape = array.shape
    index_at = [jax.random.randint(jax.random.fold_in(rng, axis), (), 0, shape[axis]) for axis in range(len(shape))]
    array = array.at[tuple(index_at)].set(low)
    longest = shape.index(max(shape))
    index_at[longest] = (index_at[longest] + 1) % shape[longest]
    return array.at[tuple(index_at)].set(high)


def level_of(key, shape, cuts, smallest, largest):
    factor_of, own = 1.0, jax.random.fold_in(key, 6)
    for dim, shards_of in cuts:
        draws = jnp.exp(jax.random.uniform(jax.random.fold_in(own, dim), (shards_of,), jnp.float32, smallest / len(cuts), largest / len(cuts)))
        factor_of = factor_of * jnp.repeat(draws, shape[dim] // shards_of).reshape([-1 if axis == dim else 1 for axis in range(len(shape))])
    return factor_of


def shared_out(rng, own, number, rows, count, top, most, slope):
    ranking = jax.random.permutation(rng, count)
    heavy_load, usual = portions_of(count, rows * top, most, slope, True), portions_of(count, rows * top, most, slope, False)
    places = jnp.arange(count)

    def named(tallies, turn):
        used = int((tallies > 0).sum())
        fixed = max(1, used // 4)
        shifted = fixed + (places - fixed + turn * (used - fixed)) % max(1, count - fixed)
        return jnp.zeros((count,), jnp.int32).at[ranking[jnp.where(places < fixed, places, shifted)]].set(jnp.asarray(tallies, jnp.int32))

    tallies = jnp.where(number % 4 == 0, named(heavy_load, number // 4), named(usual, number - number // 4 - 1))
    mixed = jax.random.permutation(jax.random.fold_in(own, 3), count)
    giver, sink = mixed[0:count // 2 * 2:2], mixed[1:count // 2 * 2:2]
    room = jnp.minimum(tallies[giver] - 1, most - tallies[sink]) // 2
    room = jnp.where((giver == ranking[0]) | (sink == ranking[0]) | (tallies[sink] == 0), 0, jnp.maximum(room, 0))
    shifted = jax.random.randint(jax.random.fold_in(own, 4), (count // 2,), 0, 1 << 20) % (room + 1)
    tallies = tallies.at[giver].add(-shifted).at[sink].add(shifted)
    labels = jnp.searchsorted(jnp.cumsum(tallies), jnp.arange(rows * top), side="right").astype(jnp.int32)
    table = labels.reshape(top, rows).T
    table = table[jax.random.permutation(jax.random.fold_in(own, 1), rows)]
    turn = jax.random.randint(jax.random.fold_in(own, 2), (rows, 1), 0, top)
    return jnp.take_along_axis(table, (jnp.arange(top)[None, :] + turn) % top, axis=1)


def portions_of(number_of, total, bound, slope, full):
    loads = [(1 << 20) // math.isqrt(standing ** slope) + 1 for standing in range(1, number_of + 1)]
    largest = bound if full else min(bound, max(-(-total // number_of), total * loads[0] // sum(loads)))
    least = 1 if total - largest >= number_of - 1 else 0
    holding, rest = [largest] + [least] * (number_of - 1), total - largest - least * (number_of - 1)
    while rest > 0:
        candidates = [i for i in range(1, number_of) if holding[i] < largest] or [i for i in range(1, number_of) if holding[i] < bound]
        mass, budget = sum([loads[i] for i in candidates]), rest
        for i in candidates:
            more = min(bound - holding[i], max(1, budget * loads[i] // mass), rest)
            holding[i] = holding[i] + more
            rest = rest - more
    return np.array(holding)


def scatter_about(rng, dims, width, reach, cuts=(), kind=jnp.bfloat16):
    loudness = level_of(rng, dims, cuts, -0.22, 0.18) if cuts else 1.0
    values = jax.random.normal(rng, dims, jnp.float32) * width * loudness
    return jnp.minimum(jnp.maximum(values, -reach), reach).astype(kind)


def setup_inputs(seed: int = 0) -> dict:
    streams_of = jax.random.split(jax.random.key(seed), 9)
    cam_jac = scatter_about(streams_of[0], (NPB, 12, TOP * BLOCK), (8 * OBS_CAM) ** -0.5, 0.125, ((0, 32),))
    point_jac = scatter_about(streams_of[1], (NPB, 6, TOP * BLOCK), (2 * TOP) ** -0.5, 1.5, ((0, 32),))
    residual = scatter_about(streams_of[2], (NPB, 2, TOP * BLOCK), 1.0, 6.0, ((0, 32),), jnp.float32)
    obs_cam_keys = jax.random.split(jax.random.fold_in(streams_of[3], 1), NPB // PBD)
    obs_cam_turns = jax.random.permutation(jax.random.fold_in(streams_of[3], 3), NPB // PBD)
    obs_cam = jax.vmap(lambda own, number: shared_out(jax.random.fold_in(streams_of[3], 2), own, number, PBD, NCB, TOP, MOST, 2))(obs_cam_keys, obs_cam_turns).reshape((NPB, TOP))
    damp_exp = set_ends(jax.random.randint(streams_of[4], (ITERS, BLOCK), -3, 1), jax.random.fold_in(streams_of[4], 1), -3, 0).astype(jnp.int32)
    cam_step = scatter_about(streams_of[5], (NCB, CVEC), 1.0, 6.0, ((0, 8),), jnp.float32)
    diag_inverse = draw_diag_inverse(jax.random.fold_in(streams_of[8], 71), 0)
    coupling = draw_coupling(jax.random.fold_in(streams_of[8], 71), 0)
    return {"cam_jac": cam_jac, "point_jac": point_jac, "residual": residual, "obs_cam": obs_cam, "damp_exp": damp_exp, "cam_step": cam_step, "diag_inverse": diag_inverse, "coupling": coupling}


exact_mode = lax.Precision.HIGHEST


def solve_three(hessian, target):
    aa_entry = hessian[:, 0, 0]
    ab_entry = hessian[:, 0, 1]
    ac_entry = hessian[:, 0, 2]
    bb_entry = hessian[:, 1, 1]
    bc_entry = hessian[:, 1, 2]
    cc_entry = hessian[:, 2, 2]
    cof_aa = bb_entry * cc_entry - bc_entry * bc_entry
    cof_ab = ac_entry * bc_entry - ab_entry * cc_entry
    cof_ac = ab_entry * bc_entry - ac_entry * bb_entry
    cof_bb = aa_entry * cc_entry - ac_entry * ac_entry
    cof_bc = ab_entry * ac_entry - aa_entry * bc_entry
    cof_cc = aa_entry * bb_entry - ab_entry * ab_entry
    determinant = aa_entry * cof_aa + ab_entry * cof_ab + ac_entry * cof_ac
    component_a = (cof_aa * target[:, 0] + cof_ab * target[:, 1] + cof_ac * target[:, 2]) / determinant
    component_b = (cof_ab * target[:, 0] + cof_bb * target[:, 1] + cof_bc * target[:, 2]) / determinant
    component_c = (cof_ac * target[:, 0] + cof_bc * target[:, 1] + cof_cc * target[:, 2]) / determinant
    return jnp.stack([component_a, component_b, component_c], axis=1)


def eliminate(cam_jac, point_jac, residual, obs_cam, cam_all, damping):
    blocks, observers = obs_cam.shape
    span_width = residual.shape[2]
    per_block = span_width // observers
    gathered = cam_all[obs_cam.reshape(-1)]
    cam_values = gathered.reshape(blocks, observers, 6, per_block).transpose(0, 2, 1, 3).reshape(blocks, 6, span_width)
    cam_terms = cam_jac.astype(jnp.float32).reshape(blocks, 2, 6, span_width)
    misfit = residual + jnp.sum(cam_terms * cam_values[:, None], axis=2)
    point_terms = point_jac.astype(jnp.float32).reshape(blocks, 2, 3, observers, per_block)
    misfit_obs = misfit.reshape(blocks, 2, observers, per_block)
    unit_three = (lax.broadcasted_iota(jnp.int32, (3, 3), 0) == lax.broadcasted_iota(jnp.int32, (3, 3), 1)).astype(jnp.float32)
    hessian = jnp.sum(point_terms[:, :, :, None] * point_terms[:, :, None, :], axis=(1, 4)) + unit_three[None, :, :, None] * damping[None, None, None, :]
    target = jnp.sum(point_terms * misfit_obs[:, :, None], axis=(1, 3))
    solution = solve_three(hessian, target)
    projected = misfit_obs - jnp.sum(point_terms * solution[:, None, :, None, :], axis=2)
    adjoint = jnp.sum(cam_terms * projected.reshape(blocks, 2, 1, span_width), axis=1)
    adjoint = adjoint.reshape(blocks, 6, observers, per_block).transpose(0, 2, 1, 3).reshape(blocks * observers, 6 * per_block)
    return adjoint, solution


def apply_panels(gradient, diag_inverse, coupling):
    cam_width = gradient.shape[1]

    def advance(carried, panels):
        inverse_block, coupling_block, grad_block = panels
        inverse_wide = inverse_block.astype(jnp.float32)
        coupling_wide = coupling_block.astype(jnp.float32)
        solved = jnp.dot(inverse_wide.T, grad_block - carried, precision=exact_mode)
        return jnp.dot(coupling_wide.T, solved, precision=exact_mode), solved

    _, solved_all = lax.scan(advance, jnp.zeros((cam_width,), jnp.float32), (diag_inverse, coupling, gradient))

    def retreat(later, panels):
        inverse_block, coupling_block, solved_block = panels
        inverse_wide = inverse_block.astype(jnp.float32)
        coupling_wide = coupling_block.astype(jnp.float32)
        update = jnp.dot(inverse_wide, solved_block - jnp.dot(coupling_wide, later, precision=exact_mode), precision=exact_mode)
        return update, update

    _, updates = lax.scan(retreat, jnp.zeros((cam_width,), jnp.float32), (diag_inverse, coupling, solved_all), reverse=True)
    return updates


def reference(cam_jac, point_jac, residual, obs_cam, damp_exp, cam_step, diag_inverse, coupling):
    total_blocks = cam_step.shape[0]
    flat_ids = obs_cam.reshape(-1)
    dampings = jnp.exp2(damp_exp.astype(jnp.float32))
    camera = cam_step
    for iteration in range(ITERS):
        damp_row = dampings[iteration]
        adjoint, _ = eliminate(cam_jac, point_jac, residual, obs_cam, camera, damp_row)
        cam_damp = jnp.tile(damp_row, 6)
        gradient = jax.ops.segment_sum(adjoint, flat_ids, num_segments=total_blocks) + cam_damp[None, :] * camera
        camera = camera - apply_panels(gradient, diag_inverse, coupling)
    _, solution = eliminate(cam_jac, point_jac, residual, obs_cam, camera, dampings[ITERS - 1])
    return camera, -solution
```

```python
import functools

import jax
import jax.numpy as jnp
from jax import lax
from jax.experimental import pallas as pl
from jax.experimental.pallas import tpu as pltpu
from jax.sharding import PartitionSpec as P

ITERS = 2
MESH = pl.DeviceIdType.MESH
F32, BF16 = jnp.float32, jnp.bfloat16
VMEM = pl.BlockSpec(memory_space=pltpu.VMEM)
ANY = pl.BlockSpec(memory_space=pl.ANY)


def dot_rows(x, panel):
    return lax.dot_general(x, panel, (((1,), (0,)), ((), ())), preferred_element_type=F32)


def dot_cols(x, panel):
    return lax.dot_general(x, panel, (((1,), (1,)), ((), ())), preferred_element_type=F32)


def halves(x):
    high = x.astype(BF16)
    return high, (x - high.astype(F32)).astype(BF16)


def thirds(x):
    high = x.astype(BF16)
    rest = x - high.astype(F32)
    mid = rest.astype(BF16)
    return high, mid, (rest - mid.astype(F32)).astype(BF16)


def eliminate(adjoint_out, cameras, pick_ref, pick_t_ref, cj_ref, pj_ref, res_ref, damp, out_ref, seen, parts):
    rows = res_ref.shape[1]
    blocks = rows // 4
    high, mid, low = thirds(cameras)
    pick = pick_ref[...]
    seen[...] = (dot_rows(pick, low) + dot_rows(pick, mid)) + dot_rows(pick, high)
    step = 16
    left = lax.broadcasted_iota(jnp.int32, (step, 128), 1) < 64

    def swap(x):
        return pltpu.roll(x, 64, 1)

    def chunk(i, carry):
        at = pl.multiple_of(i * step, step)
        misfits, points = [], []
        hess = [None] * 6
        target = [None] * 3
        pairs = ((0, 0), (0, 1), (0, 2), (1, 1), (1, 2), (2, 2))
        for tp in range(4):
            here = pl.ds(tp * blocks + at, step)
            there = pl.ds(rows + tp * blocks + at, step)
            cams = []
            for c in range(3):
                even = seen[here, c * 128 : (c + 1) * 128]
                odd = seen[there, c * 128 : (c + 1) * 128]
                cams.append(jnp.where(left, even, swap(odd)))
                cams.append(jnp.where(left, swap(even), odd))
            for a in range(2):
                miss = res_ref[a, here, :]
                for m in range(6):
                    miss = miss + cj_ref[6 * a + m, here, :].astype(F32) * cams[m]
                terms = [pj_ref[3 * a + n, here, :].astype(F32) for n in range(3)]
                misfits.append(miss)
                points.append(terms)
                for e, (n, k) in enumerate(pairs):
                    new = terms[n] * terms[k]
                    hess[e] = new if hess[e] is None else hess[e] + new
                for n in range(3):
                    new = terms[n] * miss
                    target[n] = new if target[n] is None else target[n] + new
        hess = [h + swap(h) for h in hess]
        ta, tb, tc = [t + swap(t) for t in target]
        aa, ab, ac, bb, bc, cc = hess
        aa, bb, cc = aa + damp, bb + damp, cc + damp
        cof_aa = bb * cc - bc * bc
        cof_ab = ac * bc - ab * cc
        cof_ac = ab * bc - ac * bb
        cof_bb = aa * cc - ac * ac
        cof_bc = ab * ac - aa * bc
        cof_cc = aa * bb - ab * ab
        det = aa * cof_aa + ab * cof_ab + ac * cof_ac
        sol = (
            (cof_aa * ta + cof_ab * tb + cof_ac * tc) / det,
            (cof_ab * ta + cof_bb * tb + cof_bc * tc) / det,
            (cof_ac * ta + cof_bc * tb + cof_cc * tc) / det,
        )
        if not adjoint_out:
            for n in range(3):
                out_ref[n, pl.ds(at, step), :] = -sol[n]
            return carry
        for tp in range(4):
            here = pl.ds(tp * blocks + at, step)
            there = pl.ds(rows + tp * blocks + at, step)
            left_over = []
            for a in range(2):
                terms = points[2 * tp + a]
                left_over.append(
                    misfits[2 * tp + a]
                    - (terms[0] * sol[0] + terms[1] * sol[1] + terms[2] * sol[2])
                )
            adj = [
                cj_ref[m, here, :].astype(F32) * left_over[0]
                + cj_ref[6 + m, here, :].astype(F32) * left_over[1]
                for m in range(6)
            ]
            for c in range(3):
                span = slice(c * 128, (c + 1) * 128)
                even = jnp.where(left, adj[2 * c], swap(adj[2 * c + 1]))
                odd = jnp.where(left, swap(adj[2 * c]), adj[2 * c + 1])
                for part, value in enumerate(thirds(even)):
                    parts[part, here, span] = value
                for part, value in enumerate(thirds(odd)):
                    parts[part, there, span] = value
        return carry

    lax.fori_loop(0, blocks // step, chunk, 0)
    if adjoint_out:
        pick_t = pick_t_ref[...]
        out_ref[...] = (
            dot_rows(pick_t, parts[2]) + dot_rows(pick_t, parts[1])
        ) + dot_rows(pick_t, parts[0])


def split_row(v):
    row = lax.broadcasted_iota(jnp.int32, v.shape, 0)
    high = v.astype(BF16).astype(F32)
    rest = v - high
    mid = rest.astype(BF16).astype(F32)
    low = rest - mid
    return jnp.where(row == 0, high, jnp.where(row == 1, mid, jnp.where(row == 2, low, 0.0))).astype(BF16)


def total(y):
    return jnp.broadcast_to(jnp.sum(y, axis=0, keepdims=True), y.shape)


def times(v, panel):
    return total(dot_rows(split_row(v), panel))


def times_t(v, panel):
    return total(dot_cols(split_row(v), panel))


def stacked(dot, x, panel):
    rows = x.shape[0]
    both = dot(jnp.concatenate(halves(x), axis=0), panel)
    return both[:rows] + both[rows:]


def whole_kernel(
    n_c, n_p,
    order_ref, cam_ref, damp_ref, cj_hbm, pj_hbm, res_hbm, d_hbm, c_hbm,
    cam_out, point_out,
    cj_ref, pj_ref, res_ref, d_ref, c_ref, wh_ref, wl_ref, xh_ref, xl_ref, rh_ref, rl_ref, run_f, run_b,
    pick, pick_t, seen, parts, dense, own, every,
    landed, piece, grad, solved, update, carry_in, carry_out, first_in, first_out, entry,
    run_nb, nh_ref, nl_ref, ph_ref, pk_ref,
    load_sem, rs_send, rs_recv, pts_send, pts_recv, ring_send, ring_recv, first_send, first_recv, all_send, all_recv, nb_send, nb_recv,
):
    me_c, me_p = lax.axis_index("chain"), lax.axis_index("pts")
    count, width = cam_ref.shape
    rows = res_ref.shape[1]
    loads = [
        pltpu.make_async_copy(src, dst, load_sem.at[i])
        for i, (src, dst) in enumerate(
            ((d_hbm, d_ref), (c_hbm, c_ref), (cj_hbm, cj_ref), (pj_hbm, pj_ref), (res_hbm, res_ref))
        )
    ]
    for load in loads:
        load.start()

    barrier = pltpu.get_barrier_semaphore()

    @pl.loop(1, n_c)
    def _(i):
        pl.semaphore_signal(
            barrier, inc=1, device_id=(lax.rem(me_c + i, n_c), me_p), device_id_type=MESH
        )

    for i in range(1, n_p):
        pl.semaphore_signal(
            barrier, inc=1, device_id=(me_c, lax.rem(me_p + i, n_p)), device_id_type=MESH
        )
    pl.semaphore_wait(barrier, n_c + n_p - 2)

    def all_copy(turn, i):
        return pltpu.make_async_remote_copy(
            src_ref=own.at[turn],
            dst_ref=every.at[turn, me_c],
            send_sem=all_send.at[turn, i],
            recv_sem=all_recv.at[turn, i],
            device_id=(lax.rem(me_c + i, n_c), me_p),
            device_id_type=MESH,
        )

    def share_camera(turn):
        @pl.loop(1, n_c)
        def _(i):
            all_copy(turn, i).start()

        every[turn, me_c] = own[turn]

    def await_cameras(turn):
        @pl.loop(1, n_c)
        def _(i):
            all_copy(turn, i).wait()

    own[0] = cam_ref[...]
    share_camera(0)

    cams = lax.broadcasted_iota(jnp.int32, pick_t.shape, 0)
    chosen = jnp.where(cams == jnp.broadcast_to(order_ref[...], pick_t.shape), 1.0, 0.0)
    pick_t[...] = chosen.astype(BF16)
    pick[...] = chosen.T.astype(BF16)

    unit = (
        lax.broadcasted_iota(jnp.int32, (width, width), 0)
        == lax.broadcasted_iota(jnp.int32, (width, width), 1)
    ).astype(F32)
    run_f[...] = unit
    run_b[...] = unit

    def map_ahead(k, carry):
        made = -stacked(dot_rows, run_f[...], d_ref[k])
        high, low = halves(made)
        wh_ref[k] = high
        wl_ref[k] = low
        run_f[...] = stacked(dot_rows, made, c_ref[k])
        return carry

    def map_back(i, carry):
        k = count - 1 - i
        made = stacked(dot_cols, -stacked(dot_cols, run_b[...], c_ref[k]), d_ref[k])
        run_b[...] = made
        high, low = halves(made)
        xh_ref[k] = high
        xl_ref[k] = low
        return carry

    odd = lax.rem(me_c, 2)
    swap_maps = pltpu.make_async_remote_copy(
        src_ref=run_f, dst_ref=run_nb, send_sem=nb_send, recv_sem=nb_recv,
        device_id=(me_c + 1 - 2 * odd, me_p), device_id_type=MESH,
    )

    def pair_map():
        high, low = halves(run_f[...])
        rh_ref[...] = high
        rl_ref[...] = low
        swap_maps.wait()
        mine, other = run_f[...], run_nb[...]
        nh_ref[...], nl_ref[...] = halves(other)
        early = jnp.where(odd == 1, other, mine)
        late_high, late_low = halves(jnp.where(odd == 1, mine, other))
        high, low = halves(stacked(dot_rows, early, late_high) + stacked(dot_rows, early, late_low))
        ph_ref[...] = high
        pk_ref[...] = low

    loads[0].wait()
    loads[1].wait()
    lax.fori_loop(0, count, map_ahead, 0)
    swap_maps.start()
    for load in loads[2:]:
        load.wait()
    await_cameras(0)

    def zero_ahead():
        carried = None
        for k in range(count):
            g = jnp.broadcast_to(grad[k : k + 1, :], carry_in.shape[2:])
            s = times(g if carried is None else g - carried, d_ref[k])
            solved[k : k + 1, :] = s[0:1]
            if k < count - 1:
                carried = times(s, c_ref[k])

    def zero_back():
        later = None
        for k in reversed(range(count)):
            r = jnp.broadcast_to(solved[k : k + 1, :], carry_in.shape[2:])
            if later is not None:
                r = r - times_t(later, c_ref[k])
            later = times_t(r, d_ref[k])
            update[k : k + 1, :] = later[0:1]

    def reach(vectors, high_ref, low_ref):
        acc = None
        for k in range(count):
            x = split_row(jnp.broadcast_to(vectors[k : k + 1, :], carry_in.shape[2:]))
            new = dot_cols(x, high_ref[k]) + dot_cols(x, low_ref[k])
            acc = new if acc is None else acc + new
        return -total(acc)

    def correct(x, out, high_ref, low_ref):
        for k in range(count):
            y = dot_rows(x, high_ref[k]) + dot_rows(x, low_ref[k])
            out[k : k + 1, :] = out[k : k + 1, :] + jnp.sum(y, axis=0, keepdims=True)

    def inner_step(it, carry):
        damp = damp_ref[it]
        cameras = every[it].reshape(n_c * count, width)
        eliminate(True, cameras, pick, pick_t, cj_ref, pj_ref, res_ref, damp[:, :128], dense, seen, parts)

        def rs_copy(i):
            to = lax.rem(me_c + i, n_c)
            return pltpu.make_async_remote_copy(
                src_ref=dense.at[pl.ds(pl.multiple_of(to * count, count), count)],
                dst_ref=landed.at[it, i],
                send_sem=rs_send.at[it, i],
                recv_sem=rs_recv.at[it, i],
                device_id=(to, me_p),
                device_id_type=MESH,
            )

        @pl.loop(1, n_c)
        def _(i):
            rs_copy(i).start()

        landed[it, 0] = dense[pl.ds(pl.multiple_of(me_c * count, count), count), :]

        @pl.when(it == 0)
        def _():
            lax.fori_loop(0, count, map_back, 0)

        @pl.loop(1, n_c)
        def _(i):
            rs_copy(i).wait()

        mine = jnp.sum(landed[it], axis=0)

        def pts_copy(i):
            return pltpu.make_async_remote_copy(
                src_ref=piece.at[it, me_p],
                dst_ref=piece.at[it, me_p],
                send_sem=pts_send.at[it, i],
                recv_sem=pts_recv.at[it, i],
                device_id=(me_c, lax.rem(me_p + i, n_p)),
                device_id_type=MESH,
            )

        piece[it, me_p] = mine
        for i in range(1, n_p):
            pts_copy(i).start()

        @pl.when(it == 0)
        def _():
            pair_map()

        for i in range(1, n_p):
            pts_copy(i).wait()
        grad[...] = jnp.sum(piece[it], axis=0) + damp * own[it]

        def hand(way):
            return pltpu.make_async_remote_copy(
                src_ref=first_out.at[it, way], dst_ref=first_in.at[it, way],
                send_sem=first_send.at[it, way], recv_sem=first_recv.at[it, way],
                device_id=(me_c + 1 - 2 * odd, me_p), device_id_type=MESH,
            )

        def ring(way, far):
            to = lax.rem(me_c + (n_c - far if way else far), n_c)
            return pltpu.make_async_remote_copy(
                src_ref=carry_out.at[it, way], dst_ref=carry_in.at[it, way],
                send_sem=ring_send.at[it, way, far - 1], recv_sem=ring_recv.at[it, way],
                device_id=(to, me_p), device_id_type=MESH,
            )

        def seat(way):
            turn = n_c - 1 - me_c if way else me_c
            return lax.rem(turn, 2) == 1, turn // 2

        def pass_on(way, reached, map_high, map_low, sweep):
            second, group = seat(way)
            dot = dot_cols if way else dot_rows

            def arrive():
                @pl.when(group == 0)
                def _():
                    carry_in[it, way] = jnp.zeros(carry_in.shape[2:], F32)

                @pl.when(group > 0)
                def _():
                    ring(way, 2).wait_recv()

                return carry_in[it, way]

            first_out[it, way] = reached

            @pl.when(jnp.logical_not(second))
            def _():
                hand(way).start()
                sweep()
                entry[...] = arrive()

            @pl.when(second)
            def _():
                @pl.when(group >= 2)
                def _():
                    sweep()

                hand(way).wait_recv()
                given = first_in[it, way]
                x = split_row(given)
                both = first_out[it, way] + total(dot_rows(x, map_high[...]) + dot_rows(x, map_low[...]))
                x = split_row(arrive())
                carry_out[it, way] = both + total(dot(x, ph_ref[...]) + dot(x, pk_ref[...]))

                @pl.when(group < n_c // 2 - 1)
                def _():
                    ring(way, 2).start()
                    ring(way, 1).start()

                entry[...] = given + total(dot(x, nh_ref[...]) + dot(x, nl_ref[...]))

                @pl.when(group < 2)
                def _():
                    sweep()

            return split_row(entry[...])

        def drain(way):
            second, group = seat(way)

            @pl.when(jnp.logical_not(second))
            def _():
                hand(way).wait_send()

            @pl.when(jnp.logical_and(second, group < n_c // 2 - 1))
            def _():
                ring(way, 2).wait_send()
                ring(way, 1).wait_send()

        x = pass_on(0, reach(grad, xh_ref, xl_ref), rh_ref, rl_ref, zero_ahead)
        correct(x, solved, wh_ref, wl_ref)
        x = pass_on(1, reach(solved, wh_ref, wl_ref), xh_ref.at[0], xl_ref.at[0], zero_back)
        correct(x, update, xh_ref, xl_ref)
        own[it + 1] = own[it] - update[...]
        share_camera(it + 1)

        drain(0)
        drain(1)
        await_cameras(it + 1)
        return carry

    lax.fori_loop(0, ITERS, inner_step, 0)
    cam_out[...] = own[ITERS]
    cameras = every[ITERS].reshape(n_c * count, width)
    eliminate(
        False, cameras, pick, pick_t, cj_ref, pj_ref, res_ref, damp_ref[ITERS - 1][:, :128], point_out, seen, parts
    )


def shards(n_c, n_p, cam_jac, point_jac, residual, obs_cam, damp_exp, cam_step, diag_inverse, coupling):
    blocks, observers = obs_cam.shape
    count, width = cam_step.shape
    total_blocks = count * n_c
    pairs = observers // 2
    rows = pairs * blocks

    def by_pair(x):
        comps = x.shape[1]
        return x.reshape(blocks, comps, pairs, 128).transpose(1, 2, 0, 3).reshape(comps, rows, 128)

    cj, pj, res = by_pair(cam_jac), by_pair(point_jac), by_pair(residual)
    order = obs_cam.reshape(blocks, pairs, 2).transpose(2, 1, 0).reshape(1, -1)
    wide = jnp.tile(jnp.exp2(damp_exp.astype(F32)), (1, 6))[:, None, :]
    panel = pltpu.VMEM((count, width, width), BF16)
    square = (width, width)
    sem = pltpu.SemaphoreType.DMA
    camera, out = pl.pallas_call(
        functools.partial(whole_kernel, n_c, n_p),
        in_specs=[VMEM] * 3 + [ANY] * 5,
        out_specs=[VMEM, VMEM],
        out_shape=[
            jax.ShapeDtypeStruct((count, width), F32),
            jax.ShapeDtypeStruct((3, blocks, 128), F32),
        ],
        scratch_shapes=[pltpu.VMEM(x.shape, x.dtype) for x in (cj, pj, res)]
        + [panel] * 6
        + [pltpu.VMEM(square, BF16)] * 2
        + [pltpu.VMEM(square, F32)] * 2
        + [
            pltpu.VMEM((2 * rows, total_blocks), BF16),
            pltpu.VMEM((total_blocks, 2 * rows), BF16),
            pltpu.VMEM((2 * rows, width), F32),
            pltpu.VMEM((3, 2 * rows, width), BF16),
            pltpu.VMEM((total_blocks, width), F32),
            pltpu.VMEM((ITERS + 1, count, width), F32),
            pltpu.VMEM((ITERS + 1, n_c, count, width), F32),
            pltpu.VMEM((ITERS, n_c, count, width), F32),
            pltpu.VMEM((ITERS, n_p, count, width), F32),
            pltpu.VMEM((count, width), F32),
            pltpu.VMEM((count, width), F32),
            pltpu.VMEM((count, width), F32),
            pltpu.VMEM((ITERS, 2, 8, width), F32),
            pltpu.VMEM((ITERS, 2, 8, width), F32),
            pltpu.VMEM((ITERS, 2, 8, width), F32),
            pltpu.VMEM((ITERS, 2, 8, width), F32),
            pltpu.VMEM((8, width), F32),
            pltpu.VMEM(square, F32),
            pltpu.VMEM(square, BF16),
            pltpu.VMEM(square, BF16),
            pltpu.VMEM(square, BF16),
            pltpu.VMEM(square, BF16),
            sem((5,)), sem((ITERS, n_c)), sem((ITERS, n_c)), sem((ITERS, n_p)), sem((ITERS, n_p)),
            sem((ITERS, 2, 2)), sem((ITERS, 2)), sem((ITERS, 2)), sem((ITERS, 2)),
            sem((ITERS + 1, n_c)), sem((ITERS + 1, n_c)), sem(()), sem(()),
        ],
        compiler_params=pltpu.CompilerParams(
            collective_id=0, has_side_effects=True, vmem_limit_bytes=48 << 20
        ),
        name="camera_steps",
    )(order, cam_step, wide, cj, pj, res, diag_inverse, coupling)
    return camera, out[:, :, :64].transpose(1, 0, 2)


def lanes(x, c):
    return x[:, c * 128 : (c + 1) * 128]


def to_column(x):
    return jnp.concatenate(
        [jnp.broadcast_to(lanes(x, c), (128, 128)).T for c in range(x.shape[1] // 128)], axis=0
    )


def column_times(column, m):
    return jnp.concatenate(
        [jnp.sum(m[:, c * 128 : (c + 1) * 128] * column, axis=0, keepdims=True) for c in range(m.shape[1] // 128)],
        axis=1,
    )


def spread(x, m):
    acc = None
    for c in range(m.shape[1] // 128):
        new = m[:, c * 128 : (c + 1) * 128] * lanes(x, c)
        acc = new if acc is None else acc + new
    return acc


def lane_sum(acc):
    parts = jnp.concatenate(thirds(acc), axis=1)
    return dot_cols(jnp.ones((8, parts.shape[1]), BF16), parts)[0:1]


def row_times(x, m):
    return column_times(to_column(x), m)


def row_times_t(x, m):
    return lane_sum(spread(x, m))


def eliminate_points(adjoint_out, cameras, pick_ref, pick_t_ref, cj_ref, pj_ref, res_ref, damp, out_ref, seen, parts):
    blocks = cj_ref.shape[1]
    pairs = cj_ref.shape[2] // 128
    rows = pairs * blocks
    seen[...] = dot_rows(pick_ref[...], jnp.concatenate(thirds(cameras), axis=0))
    step = 16
    left = lax.broadcasted_iota(jnp.int32, (step, 128), 1) < 64

    def swap(x):
        return pltpu.roll(x, 64, 1)

    def chunk(i, carry):
        at = pl.multiple_of(i * step, step)
        body = pl.ds(at, step)
        misfits, points = [], []
        hess = [None] * 6
        target = [None] * 3
        order = ((0, 0), (0, 1), (0, 2), (1, 1), (1, 2), (2, 2))
        for tp in range(pairs):
            here = pl.ds(tp * blocks + at, step)
            there = pl.ds(rows + tp * blocks + at, step)
            span = slice(tp * 128, (tp + 1) * 128)
            cams = []
            for c in range(3):
                even = seen[here, c * 128 : (c + 1) * 128]
                odd = seen[there, c * 128 : (c + 1) * 128]
                cams.append(jnp.where(left, even, swap(odd)))
                cams.append(jnp.where(left, swap(even), odd))
            for a in range(2):
                miss = res_ref[pl.ds(at * 2 * pairs + tp * 2 + a, step, stride=2 * pairs), :]
                for m in range(6):
                    miss = miss + cj_ref[6 * a + m, body, span].astype(F32) * cams[m]
                terms = [pj_ref[3 * a + n, body, span].astype(F32) for n in range(3)]
                misfits.append(miss)
                points.append(terms)
                for e, (n, k) in enumerate(order):
                    new = terms[n] * terms[k]
                    hess[e] = new if hess[e] is None else hess[e] + new
                for n in range(3):
                    new = terms[n] * miss
                    target[n] = new if target[n] is None else target[n] + new
        hess = [h + swap(h) for h in hess]
        ta, tb, tc = [t + swap(t) for t in target]
        aa, ab, ac, bb, bc, cc = hess
        aa, bb, cc = aa + damp, bb + damp, cc + damp
        cof_aa = bb * cc - bc * bc
        cof_ab = ac * bc - ab * cc
        cof_ac = ab * bc - ac * bb
        cof_bb = aa * cc - ac * ac
        cof_bc = ab * ac - aa * bc
        cof_cc = aa * bb - ab * ab
        det = aa * cof_aa + ab * cof_ab + ac * cof_ac
        sol = (
            (cof_aa * ta + cof_ab * tb + cof_ac * tc) / det,
            (cof_ab * ta + cof_bb * tb + cof_bc * tc) / det,
            (cof_ac * ta + cof_bc * tb + cof_cc * tc) / det,
        )
        if not adjoint_out:
            for n in range(3):
                out_ref[n, body, :] = -sol[n][:, : out_ref.shape[2]]
            return carry
        for tp in range(pairs):
            here = pl.ds(tp * blocks + at, step)
            there = pl.ds(rows + tp * blocks + at, step)
            span = slice(tp * 128, (tp + 1) * 128)
            left_over = []
            for a in range(2):
                terms = points[2 * tp + a]
                left_over.append(
                    misfits[2 * tp + a]
                    - (terms[0] * sol[0] + terms[1] * sol[1] + terms[2] * sol[2])
                )
            adj = [
                cj_ref[m, body, span].astype(F32) * left_over[0]
                + cj_ref[6 + m, body, span].astype(F32) * left_over[1]
                for m in range(6)
            ]
            for c in range(3):
                out = slice(c * 128, (c + 1) * 128)
                even = jnp.where(left, adj[2 * c], swap(adj[2 * c + 1]))
                odd = jnp.where(left, swap(adj[2 * c]), adj[2 * c + 1])
                for part, value in enumerate(halves(even)):
                    parts[part, here, out] = value
                for part, value in enumerate(halves(odd)):
                    parts[part, there, out] = value
        return carry

    lax.fori_loop(0, blocks // step, chunk, 0)
    if adjoint_out:
        pick_t = pick_t_ref[...]
        out_ref[...] = dot_rows(pick_t, parts[1]) + dot_rows(pick_t, parts[0])


def paired_kernel(
    n_c, n_p,
    obs_ref, exp_ref, cam_ref, cj_hbm, pj_hbm, res_hbm, d_hbm, c_hbm,
    cam_out, point_out,
    cj_ref, pj_ref, res_ref, d_ref, c_ref,
    w_ref, x_ref, q_ref, t_ref, e_ref, p_ref, run,
    pick, pick_t, seen, parts, dense, own, every, landed, piece, near,
    solved, update, group_f, group_b,
    load_sem, all_send, all_recv, rs_send, rs_recv, pts_send, pts_recv, near_send, near_recv,
    f_send, f_recv, b_send, b_recv, x_send, x_recv, q_send, q_recv,
    pair_send, pair_recv, core_send, core_recv, far_send, far_recv, pass_send, pass_recv,
):
    me_c, me_p = lax.axis_index("chain"), lax.axis_index("pts")
    n_g = n_c // 2
    group, odd = me_c // 2, lax.rem(me_c, 2)
    beside = me_c + 1 - 2 * odd
    twin = me_p + 1 - 2 * lax.rem(me_p, 2)
    count, width = cam_ref.shape
    half = width // 2
    mine_rows = pl.ds(pl.multiple_of(lax.rem(me_p, 2) * half, 8), half)

    barrier = pltpu.get_barrier_semaphore()

    for i in range(1, n_c):
        pl.semaphore_signal(
            barrier, inc=1, device_id=(lax.rem(me_c + i, n_c), me_p), device_id_type=MESH
        )
    for i in range(1, n_p):
        to = lax.rem(me_p + i, n_p)
        pl.semaphore_signal(barrier, inc=1, device_id=(me_c, to), device_id_type=MESH)
        pl.semaphore_signal(barrier, inc=1, device_id=(beside, to), device_id_type=MESH)

    loads = [
        pltpu.make_async_copy(src, dst, load_sem.at[i])
        for i, (src, dst) in enumerate(
            ((d_hbm, d_ref), (c_hbm, c_ref), (cj_hbm, cj_ref), (pj_hbm, pj_ref), (res_hbm, res_ref))
        )
    ]
    for load in loads:
        load.start()

    def remote(src, dst, send, recv, chain, pts):
        return pltpu.make_async_remote_copy(
            src_ref=src, dst_ref=dst, send_sem=send, recv_sem=recv,
            device_id=(chain, pts), device_id_type=MESH,
        )

    own[0] = cam_ref[...]
    obs = obs_ref[...]
    observers = obs.shape[0]
    order = jnp.concatenate(
        [obs[t : t + 1, :] for h in range(2) for t in range(h, observers, 2)], axis=1
    )
    cams = lax.broadcasted_iota(jnp.int32, pick_t.shape, 0)
    chosen = jnp.where(cams == jnp.broadcast_to(order, pick_t.shape), 1.0, 0.0)
    pick_t[...] = chosen.astype(BF16)
    pick[...] = jnp.concatenate([chosen] * 3, axis=0).T.astype(BF16)
    damps = jnp.exp2(exp_ref[...].astype(F32))
    low_damp, high_damp = damps[0:1], damps[ITERS - 1 : ITERS]

    pl.semaphore_wait(barrier, n_c - 1 + 2 * (n_p - 1))

    def all_copy(turn, i):
        return remote(
            own.at[turn], every.at[turn, me_c], all_send.at[turn, i], all_recv.at[turn, i],
            lax.rem(me_c + i, n_c), me_p,
        )

    def share_camera(turn):
        for i in range(1, n_c):
            all_copy(turn, i).start()
        every[turn, me_c] = own[turn]

    def await_cameras(turn):
        for i in range(1, n_c):
            all_copy(turn, i).wait()

    share_camera(0)

    def x_copy(k):
        return remote(x_ref.at[k, mine_rows], x_ref.at[k, mine_rows], x_send.at[k], x_recv.at[k], me_c, twin)

    def q_copy(k):
        return remote(q_ref.at[k, mine_rows], q_ref.at[k, mine_rows], q_send.at[k], q_recv.at[k], me_c, twin)

    def pair_copy(ref, i):
        return remote(ref.at[odd, mine_rows], ref.at[odd, mine_rows], pair_send.at[i], pair_recv.at[i], beside, me_p)

    def core_copy(ref, seat, i):
        return remote(ref.at[seat, mine_rows], ref.at[seat, mine_rows], core_send.at[i], core_recv.at[i], me_c, twin)

    def far_copy(i):
        to = lax.rem(group + i, n_g)
        slot = jnp.clip(group - 1, 0, n_g - 3)
        return remote(
            p_ref.at[slot, mine_rows], p_ref.at[slot, mine_rows], far_send.at[i], far_recv.at[slot],
            2 * to + odd, me_p,
        )

    def pass_copy(slot):
        return remote(
            p_ref.at[slot, mine_rows], p_ref.at[slot, mine_rows], pass_send.at[slot], pass_recv.at[slot], me_c, twin
        )

    unit_rows = (
        lax.broadcasted_iota(jnp.int32, (half, width), 0) + lax.rem(me_p, 2) * half
        == lax.broadcasted_iota(jnp.int32, (half, width), 1)
    ).astype(F32)
    run[...] = unit_rows

    def map_ahead(k, carry):
        made = -stacked(dot_rows, run[...], d_ref[k])
        w_ref[k] = made
        run[...] = stacked(dot_rows, made, c_ref[k])
        return carry

    def map_back(i, carry):
        k = count - 1 - i
        made = stacked(dot_cols, -stacked(dot_cols, run[...], c_ref[k]), d_ref[k])
        run[...] = made
        x_ref[k, mine_rows] = made
        x_copy(k).start()
        return carry

    def map_both(i, carry):
        k = count - 1 - i
        made = stacked(dot_cols, -(w_ref[k] + stacked(dot_cols, run[...], c_ref[k])), d_ref[k])
        run[...] = made
        q_ref[k, mine_rows] = made
        q_copy(k).start()
        return carry

    loads[0].wait()
    loads[1].wait()
    lax.fori_loop(0, count, map_ahead, 0)
    t_ref[odd, mine_rows] = run[...]
    pair_copy(t_ref, 0).start()
    core_copy(t_ref, odd, 0).start()
    for load in loads[2:]:
        load.wait()
    await_cameras(0)

    inner_group = jnp.logical_and(group >= 1, group <= n_g - 2)

    def broad(row):
        return jnp.broadcast_to(row, (8, width))

    def zero_ahead(grad):
        carried = None
        for k in range(count):
            g = broad(grad[k : k + 1, :])
            s = times(g if carried is None else g - carried, d_ref[k])
            solved[k : k + 1, :] = s[0:1]
            if k < count - 1:
                carried = times(s, c_ref[k])

    def zero_back():
        later = None
        for k in reversed(range(count)):
            r = broad(solved[k : k + 1, :])
            if later is not None:
                r = r - times_t(later, c_ref[k])
            later = times_t(r, d_ref[k])
            update[k : k + 1, :] = later[0:1]

    def pick_odd(if_odd, if_even):
        return jnp.where(odd == 1, if_odd, if_even)

    def inner_step(it, carry):
        first = it == 0
        damp = jnp.where(first, low_damp, high_damp)
        cameras = every[it].reshape(n_c * count, width)
        eliminate_points(
            True, cameras, pick, pick_t, cj_ref, pj_ref, res_ref,
            jnp.concatenate([damp] * 2, axis=1), dense, seen, parts,
        )

        def rs_copy(i):
            to = lax.rem(me_c + i, n_c)
            return remote(
                dense.at[pl.ds(pl.multiple_of(to * count, count), count)], landed.at[it, i],
                rs_send.at[it, i], rs_recv.at[it, i], to, me_p,
            )

        for i in range(1, n_c):
            rs_copy(i).start()
        landed[it, 0] = dense[pl.ds(pl.multiple_of(me_c * count, count), count), :]

        @pl.when(first)
        def _():
            run[...] = unit_rows
            lax.fori_loop(0, count, map_back, 0)
            run[...] = jnp.zeros(run.shape, F32)
            lax.fori_loop(0, count, map_both, 0)
            e_ref[odd, mine_rows] = run[...]
            pair_copy(e_ref, 1).start()
            core_copy(e_ref, odd, 2).start()
            pair_copy(t_ref, 0).wait()
            core_copy(t_ref, 1 - odd, 1).start()
            core_copy(t_ref, odd, 0).wait()
            core_copy(t_ref, 1 - odd, 1).wait()
            ahead = t_ref[0, mine_rows]
            high, low = halves(t_ref[1])
            made = stacked(dot_rows, ahead, high) + stacked(dot_rows, ahead, low)

            @pl.when(inner_group)
            def _():
                slot = jnp.clip(group - 1, 0, n_g - 3)
                p_ref[slot, mine_rows] = made
                pass_copy(slot).start()
                for i in range(1, n_g):
                    far_copy(i).start()

        for i in range(1, n_c):
            rs_copy(i).wait()

        wide = jnp.concatenate([damp] * (width // damp.shape[1]), axis=1)
        mine = jnp.sum(landed[it], axis=0) + jnp.where(me_p == 0, 1.0, 0.0) * (wide * own[it])

        @pl.when(first)
        def _():
            @pl.loop(0, count)
            def _(k):
                x_copy(k).wait()
                q_copy(k).wait()

        def reach(ref):
            acc = None
            for k in range(count):
                new = spread(mine[k : k + 1, :], ref.at[k])
                acc = new if acc is None else acc + new
            return lane_sum(acc)

        f_part, b_part = -reach(x_ref), reach(q_ref)
        piece[it, me_p, 0:count] = mine
        piece[it, me_p, count : count + 8] = jnp.concatenate(
            [f_part, b_part, jnp.zeros((6, width), F32)], axis=0
        )

        def near_copy(i):
            return remote(
                piece.at[it, me_p, pl.ds(count, 8)], near.at[it, me_p], near_send.at[it, i], near_recv.at[it, i],
                beside, lax.rem(me_p + i, n_p),
            )

        def pts_copy(i):
            return remote(
                piece.at[it, me_p], piece.at[it, me_p], pts_send.at[it, i], pts_recv.at[it, i],
                me_c, lax.rem(me_p + i, n_p),
            )

        for i in range(n_p):
            near_copy(i).start()
            if i:
                pts_copy(i).start()
        for i in range(n_p):
            near_copy(i).wait()
            if i:
                pts_copy(i).wait()

        both = jnp.sum(piece[it], axis=0)
        other = jnp.sum(near[it], axis=0)
        f_own, b_own = both[count : count + 1], both[count + 1 : count + 2]
        f_other, b_other = other[0:1], other[1:2]
        f_a, f_b = pick_odd(f_other, f_own), pick_odd(f_own, f_other)
        b_a, b_b = pick_odd(b_other, b_own), pick_odd(b_own, b_other)

        def group_copy(ref, send, recv, i):
            return remote(
                ref.at[it, group], ref.at[it, group], send.at[it, i], recv.at[it, i],
                2 * lax.rem(group + i, n_g) + odd, me_p,
            )

        group_f[it, group] = broad(row_times(f_a, t_ref.at[1]) + f_b)
        for i in range(1, n_g):
            group_copy(group_f, f_send, f_recv, i).start()

        zero_ahead(both)

        @pl.when(first)
        def _():
            pair_copy(e_ref, 1).wait()
            core_copy(e_ref, 1 - odd, 3).start()

            @pl.when(inner_group)
            def _():
                for i in range(1, n_g):
                    far_copy(i).wait_send()

            for slot in range(n_g - 2):
                @pl.when(group != slot + 1)
                def _():
                    remote(
                        p_ref.at[slot, mine_rows], p_ref.at[slot, mine_rows], far_send.at[0], far_recv.at[slot],
                        beside, me_p,
                    ).wait_recv()
                    pass_copy(slot).start()

            core_copy(e_ref, odd, 2).wait()
            core_copy(e_ref, 1 - odd, 3).wait()
            for slot in range(n_g - 2):
                pass_copy(slot).wait()

        for i in range(1, n_g):
            group_copy(group_f, f_send, f_recv, i).wait()

        level = group_f[it, 0][0:1]
        entered = jnp.where(group == 1, level, 0.0)
        for j in range(1, n_g - 1):
            level = group_f[it, j][0:1] + row_times(level, p_ref.at[j - 1])
            entered = jnp.where(group == j + 1, level, entered)

        column = to_column(entered)
        t_b = column_times(column, t_ref.at[0]) + f_a
        back_b = b_b - row_times(t_b, e_ref.at[1])
        back_a = b_a - column_times(column, e_ref.at[0])
        group_b[it, group] = broad(back_a + row_times_t(back_b, t_ref.at[0]))
        for i in range(1, n_g):
            group_copy(group_b, b_send, b_recv, i).start()

        zero_back()
        column = to_column(pick_odd(t_b, entered))
        fixed = update[...] - jnp.concatenate([column_times(column, q_ref.at[k]) for k in range(count)], axis=0)

        for i in range(1, n_g):
            group_copy(group_b, b_send, b_recv, i).wait()

        level = group_b[it, n_g - 1][0:1]
        entered = jnp.where(group == n_g - 2, level, 0.0)
        for j in reversed(range(1, n_g - 1)):
            level = group_b[it, j][0:1] + row_times_t(level, p_ref.at[j - 1])
            entered = jnp.where(group == j - 1, level, entered)

        later = pick_odd(entered, back_b + row_times_t(entered, t_ref.at[1]))
        column = to_column(later)
        fixed = fixed + jnp.concatenate([column_times(column, x_ref.at[k]) for k in range(count)], axis=0)
        own[it + 1] = own[it] - fixed
        share_camera(it + 1)
        await_cameras(it + 1)
        return carry

    lax.fori_loop(0, ITERS, inner_step, 0)
    cam_out[...] = own[ITERS]
    cameras = every[ITERS].reshape(n_c * count, width)
    eliminate_points(
        False, cameras, pick, pick_t, cj_ref, pj_ref, res_ref,
        jnp.concatenate([high_damp] * 2, axis=1), point_out, seen, parts,
    )


def paired_shards(n_c, n_p, cam_jac, point_jac, residual, obs_cam, damp_exp, cam_step, diag_inverse, coupling):
    blocks, observers = obs_cam.shape
    count, width = cam_step.shape
    total_blocks = count * n_c
    pairs = observers // 2
    rows = pairs * blocks
    n_g = n_c // 2
    cj, pj = cam_jac.transpose(1, 0, 2), point_jac.transpose(1, 0, 2)
    res = residual.reshape(blocks, 2, pairs, 128).transpose(0, 2, 1, 3).reshape(2 * rows, 128)
    sem = pltpu.SemaphoreType.DMA

    def vmem(*shape, dtype=F32):
        return pltpu.VMEM(shape, dtype)

    camera, out = pl.pallas_call(
        functools.partial(paired_kernel, n_c, n_p),
        in_specs=[VMEM] * 3 + [ANY] * 5,
        out_specs=[VMEM, VMEM],
        out_shape=[
            jax.ShapeDtypeStruct((count, width), F32),
            jax.ShapeDtypeStruct((3, blocks, 64), F32),
        ],
        scratch_shapes=[pltpu.VMEM(x.shape, x.dtype) for x in (cj, pj, res, diag_inverse, coupling)]
        + [
            vmem(count, width // 2, width),
            vmem(count, width, width),
            vmem(count, width, width),
            vmem(2, width, width),
            vmem(2, width, width),
            vmem(n_g - 2, width, width),
            vmem(width // 2, width),
            vmem(2 * rows, 3 * total_blocks, dtype=BF16),
            vmem(total_blocks, 2 * rows, dtype=BF16),
            vmem(2 * rows, width),
            vmem(2, 2 * rows, width, dtype=BF16),
            vmem(total_blocks, width),
            vmem(ITERS + 1, count, width),
            vmem(ITERS + 1, n_c, count, width),
            vmem(ITERS, n_c, count, width),
            vmem(ITERS, n_p, count + 8, width),
            vmem(ITERS, n_p, 8, width),
            vmem(count, width),
            vmem(count, width),
            vmem(ITERS, n_g, 8, width),
            vmem(ITERS, n_g, 8, width),
            sem((5,)), sem((ITERS + 1, n_c)), sem((ITERS + 1, n_c)), sem((ITERS, n_c)), sem((ITERS, n_c)),
            sem((ITERS, n_p)), sem((ITERS, n_p)), sem((ITERS, n_p)), sem((ITERS, n_p)),
            sem((ITERS, n_g)), sem((ITERS, n_g)), sem((ITERS, n_g)), sem((ITERS, n_g)),
            sem((count,)), sem((count,)), sem((count,)), sem((count,)),
            sem((2,)), sem((2,)), sem((4,)), sem((4,)),
            sem((n_g,)), sem((n_g - 2,)), sem((n_g - 2,)), sem((n_g - 2,)),
        ],
        compiler_params=pltpu.CompilerParams(
            collective_id=0, has_side_effects=True, vmem_limit_bytes=48 << 20
        ),
        name="camera_steps",
    )(obs_cam.T, damp_exp, cam_step, cj, pj, res, diag_inverse, coupling)
    return camera, out.transpose(1, 0, 2)


def solution(mesh):
    in_specs = (
        P(("chain", "pts"), None, None),
        P(("chain", "pts"), None, None),
        P(("chain", "pts"), None, None),
        P(("chain", "pts"), None),
        P(),
        P("chain", None),
        P("chain", None, None),
        P("chain", None, None),
    )
    out_specs = (P("chain", None), P(("chain", "pts"), None, None))
    n_c, n_p = mesh.shape["chain"], mesh.shape["pts"]
    paired = n_c % 2 == 0 and 6 <= n_c <= 16 and n_p % 2 == 0
    inner = functools.partial(paired_shards if paired else shards, n_c, n_p)
    return jax.shard_map(inner, mesh=mesh, in_specs=in_specs, out_specs=out_specs, check_vma=False)
```

```python
import functools

import jax
import jax.numpy as jnp
from jax import lax
from jax.experimental import pallas as pl
from jax.experimental.pallas import tpu as pltpu
from jax.sharding import PartitionSpec as P

ITERS = 2
MESH = pl.DeviceIdType.MESH
F32, BF16 = jnp.float32, jnp.bfloat16
VMEM = pl.BlockSpec(memory_space=pltpu.VMEM)
ANY = pl.BlockSpec(memory_space=pl.ANY)


def dot_rows(x, panel):
    return lax.dot_general(x, panel, (((1,), (0,)), ((), ())), preferred_element_type=F32)


def dot_cols(x, panel):
    return lax.dot_general(x, panel, (((1,), (1,)), ((), ())), preferred_element_type=F32)


def halves(x):
    high = x.astype(BF16)
    return high, (x - high.astype(F32)).astype(BF16)


def thirds(x):
    high = x.astype(BF16)
    rest = x - high.astype(F32)
    mid = rest.astype(BF16)
    return high, mid, (rest - mid.astype(F32)).astype(BF16)


def eliminate(adjoint_out, cameras, pick_ref, pick_t_ref, cj_ref, pj_ref, res_ref, damp, out_ref, seen, parts):
    rows = res_ref.shape[1]
    blocks = rows // 4
    high, mid, low = thirds(cameras)
    pick = pick_ref[...]
    seen[...] = (dot_rows(pick, low) + dot_rows(pick, mid)) + dot_rows(pick, high)
    step = 16
    left = lax.broadcasted_iota(jnp.int32, (step, 128), 1) < 64

    def swap(x):
        return pltpu.roll(x, 64, 1)

    def chunk(i, carry):
        at = pl.multiple_of(i * step, step)
        misfits, points = [], []
        hess = [None] * 6
        target = [None] * 3
        pairs = ((0, 0), (0, 1), (0, 2), (1, 1), (1, 2), (2, 2))
        for tp in range(4):
            here = pl.ds(tp * blocks + at, step)
            there = pl.ds(rows + tp * blocks + at, step)
            cams = []
            for c in range(3):
                even = seen[here, c * 128 : (c + 1) * 128]
                odd = seen[there, c * 128 : (c + 1) * 128]
                cams.append(jnp.where(left, even, swap(odd)))
                cams.append(jnp.where(left, swap(even), odd))
            for a in range(2):
                miss = res_ref[a, here, :]
                for m in range(6):
                    miss = miss + cj_ref[6 * a + m, here, :].astype(F32) * cams[m]
                terms = [pj_ref[3 * a + n, here, :].astype(F32) for n in range(3)]
                misfits.append(miss)
                points.append(terms)
                for e, (n, k) in enumerate(pairs):
                    new = terms[n] * terms[k]
                    hess[e] = new if hess[e] is None else hess[e] + new
                for n in range(3):
                    new = terms[n] * miss
                    target[n] = new if target[n] is None else target[n] + new
        hess = [h + swap(h) for h in hess]
        ta, tb, tc = [t + swap(t) for t in target]
        aa, ab, ac, bb, bc, cc = hess
        aa, bb, cc = aa + damp, bb + damp, cc + damp
        cof_aa = bb * cc - bc * bc
        cof_ab = ac * bc - ab * cc
        cof_ac = ab * bc - ac * bb
        cof_bb = aa * cc - ac * ac
        cof_bc = ab * ac - aa * bc
        cof_cc = aa * bb - ab * ab
        det = aa * cof_aa + ab * cof_ab + ac * cof_ac
        sol = (
            (cof_aa * ta + cof_ab * tb + cof_ac * tc) / det,
            (cof_ab * ta + cof_bb * tb + cof_bc * tc) / det,
            (cof_ac * ta + cof_bc * tb + cof_cc * tc) / det,
        )
        if not adjoint_out:
            for n in range(3):
                out_ref[n, pl.ds(at, step), :] = -sol[n]
            return carry
        for tp in range(4):
            here = pl.ds(tp * blocks + at, step)
            there = pl.ds(rows + tp * blocks + at, step)
            left_over = []
            for a in range(2):
                terms = points[2 * tp + a]
                left_over.append(
                    misfits[2 * tp + a]
                    - (terms[0] * sol[0] + terms[1] * sol[1] + terms[2] * sol[2])
                )
            adj = [
                cj_ref[m, here, :].astype(F32) * left_over[0]
                + cj_ref[6 + m, here, :].astype(F32) * left_over[1]
                for m in range(6)
            ]
            for c in range(3):
                span = slice(c * 128, (c + 1) * 128)
                even = jnp.where(left, adj[2 * c], swap(adj[2 * c + 1]))
                odd = jnp.where(left, swap(adj[2 * c]), adj[2 * c + 1])
                for part, value in enumerate(thirds(even)):
                    parts[part, here, span] = value
                for part, value in enumerate(thirds(odd)):
                    parts[part, there, span] = value
        return carry

    lax.fori_loop(0, blocks // step, chunk, 0)
    if adjoint_out:
        pick_t = pick_t_ref[...]
        out_ref[...] = (
            dot_rows(pick_t, parts[2]) + dot_rows(pick_t, parts[1])
        ) + dot_rows(pick_t, parts[0])


def split_row(v):
    row = lax.broadcasted_iota(jnp.int32, v.shape, 0)
    high = v.astype(BF16).astype(F32)
    rest = v - high
    mid = rest.astype(BF16).astype(F32)
    low = rest - mid
    return jnp.where(row == 0, high, jnp.where(row == 1, mid, jnp.where(row == 2, low, 0.0))).astype(BF16)


def total(y):
    return jnp.broadcast_to(jnp.sum(y, axis=0, keepdims=True), y.shape)


def times(v, panel):
    return total(dot_rows(split_row(v), panel))


def times_t(v, panel):
    return total(dot_cols(split_row(v), panel))


def stacked(dot, x, panel):
    rows = x.shape[0]
    both = dot(jnp.concatenate(halves(x), axis=0), panel)
    return both[:rows] + both[rows:]


def whole_kernel(
    n_c, n_p,
    order_ref, cam_ref, damp_ref, cj_hbm, pj_hbm, res_hbm, d_hbm, c_hbm,
    cam_out, point_out,
    cj_ref, pj_ref, res_ref, d_ref, c_ref, wh_ref, wl_ref, xh_ref, xl_ref, rh_ref, rl_ref, run_f, run_b,
    pick, pick_t, seen, parts, dense, own, every,
    landed, piece, grad, solved, update, carry_in, carry_out, first_in, first_out, entry,
    run_nb, nh_ref, nl_ref, ph_ref, pk_ref,
    load_sem, rs_send, rs_recv, pts_send, pts_recv, ring_send, ring_recv, first_send, first_recv, all_send, all_recv, nb_send, nb_recv,
):
    me_c, me_p = lax.axis_index("chain"), lax.axis_index("pts")
    count, width = cam_ref.shape
    rows = res_ref.shape[1]
    loads = [
        pltpu.make_async_copy(src, dst, load_sem.at[i])
        for i, (src, dst) in enumerate(
            ((d_hbm, d_ref), (c_hbm, c_ref), (cj_hbm, cj_ref), (pj_hbm, pj_ref), (res_hbm, res_ref))
        )
    ]
    for load in loads:
        load.start()

    barrier = pltpu.get_barrier_semaphore()

    @pl.loop(1, n_c)
    def _(i):
        pl.semaphore_signal(
            barrier, inc=1, device_id=(lax.rem(me_c + i, n_c), me_p), device_id_type=MESH
        )

    for i in range(1, n_p):
        pl.semaphore_signal(
            barrier, inc=1, device_id=(me_c, lax.rem(me_p + i, n_p)), device_id_type=MESH
        )
    pl.semaphore_wait(barrier, n_c + n_p - 2)

    def all_copy(turn, i):
        return pltpu.make_async_remote_copy(
            src_ref=own.at[turn],
            dst_ref=every.at[turn, me_c],
            send_sem=all_send.at[turn, i],
            recv_sem=all_recv.at[turn, i],
            device_id=(lax.rem(me_c + i, n_c), me_p),
            device_id_type=MESH,
        )

    def share_camera(turn):
        @pl.loop(1, n_c)
        def _(i):
            all_copy(turn, i).start()

        every[turn, me_c] = own[turn]

    def await_cameras(turn):
        @pl.loop(1, n_c)
        def _(i):
            all_copy(turn, i).wait()

    own[0] = cam_ref[...]
    share_camera(0)

    cams = lax.broadcasted_iota(jnp.int32, pick_t.shape, 0)
    chosen = jnp.where(cams == jnp.broadcast_to(order_ref[...], pick_t.shape), 1.0, 0.0)
    pick_t[...] = chosen.astype(BF16)
    pick[...] = chosen.T.astype(BF16)

    unit = (
        lax.broadcasted_iota(jnp.int32, (width, width), 0)
        == lax.broadcasted_iota(jnp.int32, (width, width), 1)
    ).astype(F32)
    run_f[...] = unit
    run_b[...] = unit

    def map_ahead(k, carry):
        made = -stacked(dot_rows, run_f[...], d_ref[k])
        high, low = halves(made)
        wh_ref[k] = high
        wl_ref[k] = low
        run_f[...] = stacked(dot_rows, made, c_ref[k])
        return carry

    def map_back(i, carry):
        k = count - 1 - i
        made = stacked(dot_cols, -stacked(dot_cols, run_b[...], c_ref[k]), d_ref[k])
        run_b[...] = made
        high, low = halves(made)
        xh_ref[k] = high
        xl_ref[k] = low
        return carry

    odd = lax.rem(me_c, 2)
    swap_maps = pltpu.make_async_remote_copy(
        src_ref=run_f, dst_ref=run_nb, send_sem=nb_send, recv_sem=nb_recv,
        device_id=(me_c + 1 - 2 * odd, me_p), device_id_type=MESH,
    )

    def pair_map():
        high, low = halves(run_f[...])
        rh_ref[...] = high
        rl_ref[...] = low
        swap_maps.wait()
        mine, other = run_f[...], run_nb[...]
        nh_ref[...], nl_ref[...] = halves(other)
        early = jnp.where(odd == 1, other, mine)
        late_high, late_low = halves(jnp.where(odd == 1, mine, other))
        high, low = halves(stacked(dot_rows, early, late_high) + stacked(dot_rows, early, late_low))
        ph_ref[...] = high
        pk_ref[...] = low

    loads[0].wait()
    loads[1].wait()
    lax.fori_loop(0, count, map_ahead, 0)
    swap_maps.start()
    for load in loads[2:]:
        load.wait()
    await_cameras(0)

    def zero_ahead():
        carried = None
        for k in range(count):
            g = jnp.broadcast_to(grad[k : k + 1, :], carry_in.shape[2:])
            s = times(g if carried is None else g - carried, d_ref[k])
            solved[k : k + 1, :] = s[0:1]
            if k < count - 1:
                carried = times(s, c_ref[k])

    def zero_back():
        later = None
        for k in reversed(range(count)):
            r = jnp.broadcast_to(solved[k : k + 1, :], carry_in.shape[2:])
            if later is not None:
                r = r - times_t(later, c_ref[k])
            later = times_t(r, d_ref[k])
            update[k : k + 1, :] = later[0:1]

    def reach(vectors, high_ref, low_ref):
        acc = None
        for k in range(count):
            x = split_row(jnp.broadcast_to(vectors[k : k + 1, :], carry_in.shape[2:]))
            new = dot_cols(x, high_ref[k]) + dot_cols(x, low_ref[k])
            acc = new if acc is None else acc + new
        return -total(acc)

    def correct(x, out, high_ref, low_ref):
        for k in range(count):
            y = dot_rows(x, high_ref[k]) + dot_rows(x, low_ref[k])
            out[k : k + 1, :] = out[k : k + 1, :] + jnp.sum(y, axis=0, keepdims=True)

    def inner_step(it, carry):
        damp = damp_ref[it]
        cameras = every[it].reshape(n_c * count, width)
        eliminate(True, cameras, pick, pick_t, cj_ref, pj_ref, res_ref, damp[:, :128], dense, seen, parts)

        def rs_copy(i):
            to = lax.rem(me_c + i, n_c)
            return pltpu.make_async_remote_copy(
                src_ref=dense.at[pl.ds(pl.multiple_of(to * count, count), count)],
                dst_ref=landed.at[it, i],
                send_sem=rs_send.at[it, i],
                recv_sem=rs_recv.at[it, i],
                device_id=(to, me_p),
                device_id_type=MESH,
            )

        @pl.loop(1, n_c)
        def _(i):
            rs_copy(i).start()

        landed[it, 0] = dense[pl.ds(pl.multiple_of(me_c * count, count), count), :]

        @pl.when(it == 0)
        def _():
            lax.fori_loop(0, count, map_back, 0)

        @pl.loop(1, n_c)
        def _(i):
            rs_copy(i).wait()

        mine = jnp.sum(landed[it], axis=0)

        def pts_copy(i):
            return pltpu.make_async_remote_copy(
                src_ref=piece.at[it, me_p],
                dst_ref=piece.at[it, me_p],
                send_sem=pts_send.at[it, i],
                recv_sem=pts_recv.at[it, i],
                device_id=(me_c, lax.rem(me_p + i, n_p)),
                device_id_type=MESH,
            )

        piece[it, me_p] = mine
        for i in range(1, n_p):
            pts_copy(i).start()

        @pl.when(it == 0)
        def _():
            pair_map()

        for i in range(1, n_p):
            pts_copy(i).wait()
        grad[...] = jnp.sum(piece[it], axis=0) + damp * own[it]

        def hand(way):
            return pltpu.make_async_remote_copy(
                src_ref=first_out.at[it, way], dst_ref=first_in.at[it, way],
                send_sem=first_send.at[it, way], recv_sem=first_recv.at[it, way],
                device_id=(me_c + 1 - 2 * odd, me_p), device_id_type=MESH,
            )

        def ring(way, far):
            to = lax.rem(me_c + (n_c - far if way else far), n_c)
            return pltpu.make_async_remote_copy(
                src_ref=carry_out.at[it, way], dst_ref=carry_in.at[it, way],
                send_sem=ring_send.at[it, way, far - 1], recv_sem=ring_recv.at[it, way],
                device_id=(to, me_p), device_id_type=MESH,
            )

        def seat(way):
            turn = n_c - 1 - me_c if way else me_c
            return lax.rem(turn, 2) == 1, turn // 2

        def pass_on(way, reached, map_high, map_low, sweep):
            second, group = seat(way)
            dot = dot_cols if way else dot_rows

            def arrive():
                @pl.when(group == 0)
                def _():
                    carry_in[it, way] = jnp.zeros(carry_in.shape[2:], F32)

                @pl.when(group > 0)
                def _():
                    ring(way, 2).wait_recv()

                return carry_in[it, way]

            first_out[it, way] = reached

            @pl.when(jnp.logical_not(second))
            def _():
                hand(way).start()
                sweep()
                entry[...] = arrive()

            @pl.when(second)
            def _():
                @pl.when(group >= 2)
                def _():
                    sweep()

                hand(way).wait_recv()
                given = first_in[it, way]
                x = split_row(given)
                both = first_out[it, way] + total(dot_rows(x, map_high[...]) + dot_rows(x, map_low[...]))
                x = split_row(arrive())
                carry_out[it, way] = both + total(dot(x, ph_ref[...]) + dot(x, pk_ref[...]))

                @pl.when(group < n_c // 2 - 1)
                def _():
                    ring(way, 2).start()
                    ring(way, 1).start()

                entry[...] = given + total(dot(x, nh_ref[...]) + dot(x, nl_ref[...]))

                @pl.when(group < 2)
                def _():
                    sweep()

            return split_row(entry[...])

        def drain(way):
            second, group = seat(way)

            @pl.when(jnp.logical_not(second))
            def _():
                hand(way).wait_send()

            @pl.when(jnp.logical_and(second, group < n_c // 2 - 1))
            def _():
                ring(way, 2).wait_send()
                ring(way, 1).wait_send()

        x = pass_on(0, reach(grad, xh_ref, xl_ref), rh_ref, rl_ref, zero_ahead)
        correct(x, solved, wh_ref, wl_ref)
        x = pass_on(1, reach(solved, wh_ref, wl_ref), xh_ref.at[0], xl_ref.at[0], zero_back)
        correct(x, update, xh_ref, xl_ref)
        own[it + 1] = own[it] - update[...]
        share_camera(it + 1)

        drain(0)
        drain(1)
        await_cameras(it + 1)
        return carry

    lax.fori_loop(0, ITERS, inner_step, 0)
    cam_out[...] = own[ITERS]
    cameras = every[ITERS].reshape(n_c * count, width)
    eliminate(
        False, cameras, pick, pick_t, cj_ref, pj_ref, res_ref, damp_ref[ITERS - 1][:, :128], point_out, seen, parts
    )


def shards(n_c, n_p, cam_jac, point_jac, residual, obs_cam, damp_exp, cam_step, diag_inverse, coupling):
    blocks, observers = obs_cam.shape
    count, width = cam_step.shape
    total_blocks = count * n_c
    pairs = observers // 2
    rows = pairs * blocks

    def by_pair(x):
        comps = x.shape[1]
        return x.reshape(blocks, comps, pairs, 128).transpose(1, 2, 0, 3).reshape(comps, rows, 128)

    cj, pj, res = by_pair(cam_jac), by_pair(point_jac), by_pair(residual)
    order = obs_cam.reshape(blocks, pairs, 2).transpose(2, 1, 0).reshape(1, -1)
    wide = jnp.tile(jnp.exp2(damp_exp.astype(F32)), (1, 6))[:, None, :]
    panel = pltpu.VMEM((count, width, width), BF16)
    square = (width, width)
    sem = pltpu.SemaphoreType.DMA
    camera, out = pl.pallas_call(
        functools.partial(whole_kernel, n_c, n_p),
        in_specs=[VMEM] * 3 + [ANY] * 5,
        out_specs=[VMEM, VMEM],
        out_shape=[
            jax.ShapeDtypeStruct((count, width), F32),
            jax.ShapeDtypeStruct((3, blocks, 128), F32),
        ],
        scratch_shapes=[pltpu.VMEM(x.shape, x.dtype) for x in (cj, pj, res)]
        + [panel] * 6
        + [pltpu.VMEM(square, BF16)] * 2
        + [pltpu.VMEM(square, F32)] * 2
        + [
            pltpu.VMEM((2 * rows, total_blocks), BF16),
            pltpu.VMEM((total_blocks, 2 * rows), BF16),
            pltpu.VMEM((2 * rows, width), F32),
            pltpu.VMEM((3, 2 * rows, width), BF16),
            pltpu.VMEM((total_blocks, width), F32),
            pltpu.VMEM((ITERS + 1, count, width), F32),
            pltpu.VMEM((ITERS + 1, n_c, count, width), F32),
            pltpu.VMEM((ITERS, n_c, count, width), F32),
            pltpu.VMEM((ITERS, n_p, count, width), F32),
            pltpu.VMEM((count, width), F32),
            pltpu.VMEM((count, width), F32),
            pltpu.VMEM((count, width), F32),
            pltpu.VMEM((ITERS, 2, 8, width), F32),
            pltpu.VMEM((ITERS, 2, 8, width), F32),
            pltpu.VMEM((ITERS, 2, 8, width), F32),
            pltpu.VMEM((ITERS, 2, 8, width), F32),
            pltpu.VMEM((8, width), F32),
            pltpu.VMEM(square, F32),
            pltpu.VMEM(square, BF16),
            pltpu.VMEM(square, BF16),
            pltpu.VMEM(square, BF16),
            pltpu.VMEM(square, BF16),
            sem((5,)), sem((ITERS, n_c)), sem((ITERS, n_c)), sem((ITERS, n_p)), sem((ITERS, n_p)),
            sem((ITERS, 2, 2)), sem((ITERS, 2)), sem((ITERS, 2)), sem((ITERS, 2)),
            sem((ITERS + 1, n_c)), sem((ITERS + 1, n_c)), sem(()), sem(()),
        ],
        compiler_params=pltpu.CompilerParams(
            collective_id=0, has_side_effects=True, vmem_limit_bytes=48 << 20
        ),
        name="camera_steps",
    )(order, cam_step, wide, cj, pj, res, diag_inverse, coupling)
    return camera, out[:, :, :64].transpose(1, 0, 2)


def lanes(x, c):
    return x[:, c * 128 : (c + 1) * 128]


def to_column(x):
    return jnp.concatenate(
        [jnp.broadcast_to(lanes(x, c), (128, 128)).T for c in range(x.shape[1] // 128)], axis=0
    )


def column_times(column, m):
    return jnp.concatenate(
        [jnp.sum(m[:, c * 128 : (c + 1) * 128] * column, axis=0, keepdims=True) for c in range(m.shape[1] // 128)],
        axis=1,
    )


def spread(x, m):
    acc = None
    for c in range(m.shape[1] // 128):
        new = m[:, c * 128 : (c + 1) * 128] * lanes(x, c)
        acc = new if acc is None else acc + new
    return acc


def lane_sum(acc):
    parts = jnp.concatenate(thirds(acc), axis=1)
    return dot_cols(jnp.ones((8, parts.shape[1]), BF16), parts)[0:1]


def row_times(x, m):
    return column_times(to_column(x), m)


def row_times_t(x, m):
    return lane_sum(spread(x, m))


def eliminate_points(adjoint_out, cameras, pick_ref, pick_t_ref, cj_ref, pj_ref, res_ref, damp, out_ref, seen, parts):
    blocks = cj_ref.shape[1]
    pairs = cj_ref.shape[2] // 128
    rows = pairs * blocks
    seen[...] = dot_rows(pick_ref[...], jnp.concatenate(thirds(cameras), axis=0))
    step = 16
    left = lax.broadcasted_iota(jnp.int32, (step, 128), 1) < 64

    def swap(x):
        return pltpu.roll(x, 64, 1)

    def chunk(i, carry):
        at = pl.multiple_of(i * step, step)
        body = pl.ds(at, step)
        misfits, points = [], []
        hess = [None] * 6
        target = [None] * 3
        order = ((0, 0), (0, 1), (0, 2), (1, 1), (1, 2), (2, 2))
        for tp in range(pairs):
            here = pl.ds(tp * blocks + at, step)
            there = pl.ds(rows + tp * blocks + at, step)
            span = slice(tp * 128, (tp + 1) * 128)
            cams = []
            for c in range(3):
                even = seen[here, c * 128 : (c + 1) * 128]
                odd = seen[there, c * 128 : (c + 1) * 128]
                cams.append(jnp.where(left, even, swap(odd)))
                cams.append(jnp.where(left, swap(even), odd))
            for a in range(2):
                miss = res_ref[pl.ds(at * 2 * pairs + tp * 2 + a, step, stride=2 * pairs), :]
                for m in range(6):
                    miss = miss + cj_ref[6 * a + m, body, span].astype(F32) * cams[m]
                terms = [pj_ref[3 * a + n, body, span].astype(F32) for n in range(3)]
                misfits.append(miss)
                points.append(terms)
                for e, (n, k) in enumerate(order):
                    new = terms[n] * terms[k]
                    hess[e] = new if hess[e] is None else hess[e] + new
                for n in range(3):
                    new = terms[n] * miss
                    target[n] = new if target[n] is None else target[n] + new
        hess = [h + swap(h) for h in hess]
        ta, tb, tc = [t + swap(t) for t in target]
        aa, ab, ac, bb, bc, cc = hess
        aa, bb, cc = aa + damp, bb + damp, cc + damp
        cof_aa = bb * cc - bc * bc
        cof_ab = ac * bc - ab * cc
        cof_ac = ab * bc - ac * bb
        cof_bb = aa * cc - ac * ac
        cof_bc = ab * ac - aa * bc
        cof_cc = aa * bb - ab * ab
        det = aa * cof_aa + ab * cof_ab + ac * cof_ac
        sol = (
            (cof_aa * ta + cof_ab * tb + cof_ac * tc) / det,
            (cof_ab * ta + cof_bb * tb + cof_bc * tc) / det,
            (cof_ac * ta + cof_bc * tb + cof_cc * tc) / det,
        )
        if not adjoint_out:
            for n in range(3):
                out_ref[n, body, :] = -sol[n][:, : out_ref.shape[2]]
            return carry
        for tp in range(pairs):
            here = pl.ds(tp * blocks + at, step)
            there = pl.ds(rows + tp * blocks + at, step)
            span = slice(tp * 128, (tp + 1) * 128)
            left_over = []
            for a in range(2):
                terms = points[2 * tp + a]
                left_over.append(
                    misfits[2 * tp + a]
                    - (terms[0] * sol[0] + terms[1] * sol[1] + terms[2] * sol[2])
                )
            adj = [
                cj_ref[m, body, span].astype(F32) * left_over[0]
                + cj_ref[6 + m, body, span].astype(F32) * left_over[1]
                for m in range(6)
            ]
            for c in range(3):
                out = slice(c * 128, (c + 1) * 128)
                even = jnp.where(left, adj[2 * c], swap(adj[2 * c + 1]))
                odd = jnp.where(left, swap(adj[2 * c]), adj[2 * c + 1])
                for part, value in enumerate(halves(even)):
                    parts[part, here, out] = value
                for part, value in enumerate(halves(odd)):
                    parts[part, there, out] = value
        return carry

    lax.fori_loop(0, blocks // step, chunk, 0)
    if adjoint_out:
        pick_t = pick_t_ref[...]
        out_ref[...] = dot_rows(pick_t, parts[1]) + dot_rows(pick_t, parts[0])


def paired_kernel(
    n_c, n_p,
    obs_hbm, exp_hbm, cam_hbm, cj_hbm, pj_hbm, res_hbm, d_hbm, c_hbm,
    cam_out, point_out,
    obs_ref, exp_ref, cj_ref, pj_ref, res_ref, d_ref, c_ref,
    w_ref, x_ref, q_ref, t_ref, e_ref, p_ref, run,
    pick, pick_t, seen, parts, dense, own, every, landed, piece, near,
    solved, update, group_f, group_b, ring_out, ring_in, link,
    load_sem, panel_sem, all_send, all_recv, rs_send, rs_recv, pts_send, pts_recv, near_send, near_recv,
    f_send, f_recv, b_send, b_recv, x_send, x_recv, q_send, q_recv,
    pair_send, pair_recv, core_send, core_recv, far_send, far_recv, pass_send, pass_recv,
    ring_send, ring_recv,
):
    me_c, me_p = lax.axis_index("chain"), lax.axis_index("pts")
    n_g = n_c // 2
    group, odd = me_c // 2, lax.rem(me_c, 2)
    beside = me_c + 1 - 2 * odd
    twin = me_p + 1 - 2 * lax.rem(me_p, 2)
    count, width = cam_hbm.shape
    half = width // 2
    early = min(3, count)
    mine_rows = pl.ds(pl.multiple_of(lax.rem(me_p, 2) * half, 8), half)

    barrier = pltpu.get_barrier_semaphore()

    for i in range(1, n_c):
        pl.semaphore_signal(
            barrier, inc=1, device_id=(lax.rem(me_c + i, n_c), me_p), device_id_type=MESH
        )
    for i in range(1, n_p):
        to = lax.rem(me_p + i, n_p)
        pl.semaphore_signal(barrier, inc=1, device_id=(me_c, to), device_id_type=MESH)
        pl.semaphore_signal(barrier, inc=1, device_id=(beside, to), device_id_type=MESH)

    loads = [
        pltpu.make_async_copy(src, dst, load_sem.at[i])
        for i, (src, dst) in enumerate(
            (
                (cam_hbm, own.at[0]), (obs_hbm, obs_ref), (exp_hbm, exp_ref),
                (cj_hbm, cj_ref), (pj_hbm, pj_ref), (res_hbm, res_ref),
            )
        )
    ]

    def panel_load(k):
        return (
            pltpu.make_async_copy(d_hbm.at[k], d_ref.at[k], panel_sem.at[0, k]),
            pltpu.make_async_copy(c_hbm.at[k], c_ref.at[k], panel_sem.at[1, k]),
        )

    for k in range(count):
        for load in panel_load(k):
            load.start()
        if k == 0:
            for load in loads[:3]:
                load.start()
    for load in loads[3:]:
        load.start()

    def remote(src, dst, send, recv, chain, pts):
        return pltpu.make_async_remote_copy(
            src_ref=src, dst_ref=dst, send_sem=send, recv_sem=recv,
            device_id=(chain, pts), device_id_type=MESH,
        )

    def all_copy(turn, i):
        return remote(
            own.at[turn], every.at[turn, me_c], all_send.at[turn, i], all_recv.at[turn, i],
            lax.rem(me_c + i, n_c), me_p,
        )

    def share_camera(turn):
        for i in range(1, n_c):
            all_copy(turn, i).start()
        every[turn, me_c] = own[turn]

    def await_cameras(turn):
        for i in range(1, n_c):
            all_copy(turn, i).wait()

    def x_copy(k):
        return remote(x_ref.at[k, mine_rows], x_ref.at[k, mine_rows], x_send.at[k], x_recv.at[k], me_c, twin)

    def q_copy(k):
        return remote(q_ref.at[k, mine_rows], q_ref.at[k, mine_rows], q_send.at[k], q_recv.at[k], me_c, twin)

    def pair_copy(ref, i):
        return remote(ref.at[odd, mine_rows], ref.at[odd, mine_rows], pair_send.at[i], pair_recv.at[i], beside, me_p)

    def core_copy(ref, seat, i):
        return remote(ref.at[seat, mine_rows], ref.at[seat, mine_rows], core_send.at[i], core_recv.at[i], me_c, twin)

    own_slot = jnp.clip(group - 1, 0, n_g - 3)

    def far_each(where, act):
        for i in range(1, n_g):
            to = lax.rem(group + i, n_g)

            @pl.when(where(to))
            def _():
                act(
                    remote(
                        p_ref.at[own_slot, mine_rows], p_ref.at[own_slot, mine_rows],
                        far_send.at[i], far_recv.at[own_slot], 2 * to + odd, me_p,
                    )
                )

    def far_arrive(where):
        for slot in range(n_g - 2):
            @pl.when(where(slot + 1))
            def _():
                remote(
                    p_ref.at[slot, mine_rows], p_ref.at[slot, mine_rows], far_send.at[0], far_recv.at[slot],
                    beside, me_p,
                ).wait_recv()
                pass_copy(slot).start()

    def pass_arrive(where):
        for slot in range(n_g - 2):
            @pl.when(where(slot + 1))
            def _():
                pass_copy(slot).wait()

    def pass_copy(slot):
        return remote(
            p_ref.at[slot, mine_rows], p_ref.at[slot, mine_rows], pass_send.at[slot], pass_recv.at[slot], me_c, twin
        )

    unit_rows = (
        lax.broadcasted_iota(jnp.int32, (half, width), 0) + lax.rem(me_p, 2) * half
        == lax.broadcasted_iota(jnp.int32, (half, width), 1)
    ).astype(F32)
    run[...] = unit_rows

    def map_ahead(k, carry):
        for load in panel_load(k):
            load.wait()
        made = -stacked(dot_rows, run[...], d_ref[k])
        w_ref[k] = made
        run[...] = stacked(dot_rows, made, c_ref[k])
        return carry

    def map_back(i, carry):
        k = count - 1 - i
        made = stacked(dot_cols, -stacked(dot_cols, run[...], c_ref[k]), d_ref[k])
        run[...] = made
        x_ref[k, mine_rows] = made
        x_copy(k).start()
        return carry

    def map_both(i, carry):
        k = count - 1 - i
        made = stacked(dot_cols, -(w_ref[k] + stacked(dot_cols, run[...], c_ref[k])), d_ref[k])
        run[...] = made
        q_ref[k, mine_rows] = made
        q_copy(k).start()
        return carry

    lax.fori_loop(0, early, map_ahead, 0)

    for load in loads[:3]:
        load.wait()
    obs = obs_ref[...]
    observers = obs.shape[0]
    order = jnp.concatenate(
        [obs[t : t + 1, :] for h in range(2) for t in range(h, observers, 2)], axis=1
    )
    cams = lax.broadcasted_iota(jnp.int32, pick_t.shape, 0)
    chosen = jnp.where(cams == jnp.broadcast_to(order, pick_t.shape), 1.0, 0.0)
    pick_t[...] = chosen.astype(BF16)
    pick[...] = jnp.concatenate([chosen] * 3, axis=0).T.astype(BF16)
    damps = jnp.exp2(exp_ref[...].astype(F32))
    low_damp, high_damp = damps[0:1], damps[ITERS - 1 : ITERS]

    pl.semaphore_wait(barrier, n_c - 1 + 2 * (n_p - 1))

    share_camera(0)
    lax.fori_loop(early, count, map_ahead, 0)
    t_ref[odd, mine_rows] = run[...]
    pair_copy(t_ref, 0).start()
    core_copy(t_ref, odd, 0).start()
    run[...] = unit_rows
    lax.fori_loop(0, count, map_back, 0)
    for load in loads[3:]:
        load.wait()
    await_cameras(0)

    inner_group = jnp.logical_and(group >= 1, group <= n_g - 2)

    def broad(row):
        return jnp.broadcast_to(row, (8, width))

    def zero_ahead(grad):
        carried = None
        for k in range(count):
            g = broad(grad[k : k + 1, :])
            s = times(g if carried is None else g - carried, d_ref[k])
            solved[k : k + 1, :] = s[0:1]
            if k < count - 1:
                carried = times(s, c_ref[k])

    def zero_back():
        later = None
        for k in reversed(range(count)):
            r = broad(solved[k : k + 1, :])
            if later is not None:
                r = r - times_t(later, c_ref[k])
            later = times_t(r, d_ref[k])
            update[k : k + 1, :] = later[0:1]

    def pick_odd(if_odd, if_even):
        return jnp.where(odd == 1, if_odd, if_even)

    def inner_step(it, carry):
        first = it == 0
        damp = jnp.where(first, low_damp, high_damp)
        cameras = every[it].reshape(n_c * count, width)
        eliminate_points(
            True, cameras, pick, pick_t, cj_ref, pj_ref, res_ref,
            jnp.concatenate([damp] * 2, axis=1), dense, seen, parts,
        )

        def rs_copy(i):
            to = lax.rem(me_c + i, n_c)
            return remote(
                dense.at[pl.ds(pl.multiple_of(to * count, count), count)], landed.at[it, i],
                rs_send.at[it, i], rs_recv.at[it, i], to, me_p,
            )

        for i in range(1, n_c):
            rs_copy(i).start()
        landed[it, 0] = dense[pl.ds(pl.multiple_of(me_c * count, count), count), :]

        @pl.when(first)
        def _():
            run[...] = jnp.zeros(run.shape, F32)
            lax.fori_loop(0, count, map_both, 0)
            e_ref[odd, mine_rows] = run[...]
            core_copy(e_ref, odd, 2).start()
            pair_copy(t_ref, 0).wait()
            core_copy(t_ref, 1 - odd, 1).start()

        for i in range(1, n_c):
            rs_copy(i).wait()

        wide = jnp.concatenate([damp] * (width // damp.shape[1]), axis=1)
        mine = jnp.sum(landed[it], axis=0) + jnp.where(me_p == 0, 1.0, 0.0) * (wide * own[it])

        @pl.when(first)
        def _():
            @pl.loop(0, count)
            def _(k):
                x_copy(k).wait()
                q_copy(k).wait()

        def reach(ref):
            acc = None
            for k in range(count):
                new = spread(mine[k : k + 1, :], ref.at[k])
                acc = new if acc is None else acc + new
            return lane_sum(acc)

        f_part, b_part = -reach(x_ref), reach(q_ref)
        piece[it, me_p, 0:count] = mine
        piece[it, me_p, count : count + 8] = jnp.concatenate(
            [f_part, b_part, jnp.zeros((6, width), F32)], axis=0
        )

        def near_copy(i):
            return remote(
                piece.at[it, me_p, pl.ds(count, 8)], near.at[it, me_p], near_send.at[it, i], near_recv.at[it, i],
                beside, lax.rem(me_p + i, n_p),
            )

        def pts_copy(i):
            return remote(
                piece.at[it, me_p], piece.at[it, me_p], pts_send.at[it, i], pts_recv.at[it, i],
                me_c, lax.rem(me_p + i, n_p),
            )

        for i in range(n_p):
            near_copy(i).start()
            if i:
                pts_copy(i).start()

        @pl.when(first)
        def _():
            pair_copy(e_ref, 1).start()
            core_copy(t_ref, odd, 0).wait()
            core_copy(t_ref, 1 - odd, 1).wait()

            @pl.when(inner_group)
            def _():
                ahead = t_ref[0, mine_rows]
                high, low = halves(t_ref[1])
                p_ref[own_slot, mine_rows] = stacked(dot_rows, ahead, high) + stacked(dot_rows, ahead, low)
                pass_copy(own_slot).start()
                far_each(lambda to: to <= group + 1, lambda copy: copy.start())

        for i in range(n_p):
            near_copy(i).wait()
            if i:
                pts_copy(i).wait()

        both = jnp.sum(piece[it], axis=0)
        other = jnp.sum(near[it], axis=0)
        f_own, b_own = both[count : count + 1], both[count + 1 : count + 2]
        f_other, b_other = other[0:1], other[1:2]
        f_a, f_b = pick_odd(f_other, f_own), pick_odd(f_own, f_other)
        b_a, b_b = pick_odd(b_other, b_own), pick_odd(b_own, b_other)

        def group_copy(ref, send, recv, i):
            return remote(
                ref.at[it, group], ref.at[it, group], send.at[it, i], recv.at[it, i],
                2 * lax.rem(group + i, n_g) + odd, me_p,
            )

        group_f[it, group] = broad(row_times(f_a, t_ref.at[1]) + f_b)

        def ring_copy():
            return remote(
                ring_out, ring_in, ring_send, ring_recv, 2 * lax.rem(group + 1, n_g) + odd, me_p
            )

        def fetch_e():
            pair_copy(e_ref, 1).wait()
            core_copy(e_ref, 1 - odd, 3).start()

        @pl.when(first)
        def _():
            @pl.when(group == 0)
            def _():
                ring_out[...] = group_f[it, group]
                ring_copy().start()

        @pl.when(jnp.logical_not(first))
        def _():
            for i in range(1, n_g):
                group_copy(group_f, f_send, f_recv, i).start()

        zero_ahead(both)

        @pl.when(first)
        def _():
            @pl.when(group >= n_g // 2)
            def _():
                fetch_e()

            @pl.when(group == 0)
            def _():
                link[...] = jnp.zeros(link.shape, F32)

            @pl.when(group > 0)
            def _():
                ring_copy().wait_recv()
                link[...] = ring_in[...]

            @pl.when(inner_group)
            def _():
                pass_copy(own_slot).wait()
                ring_out[...] = group_f[it, group] + row_times(link[0:1, :], p_ref.at[own_slot])
                ring_copy().start()
                far_each(lambda to: to > group + 1, lambda copy: copy.start())

            @pl.when(group < n_g // 2)
            def _():
                fetch_e()

            core_copy(e_ref, odd, 2).wait()
            core_copy(e_ref, 1 - odd, 3).wait()

        @pl.when(jnp.logical_not(first))
        def _():
            for i in range(1, n_g):
                group_copy(group_f, f_send, f_recv, i).wait()
            link[...] = jnp.where(group == 0, 0.0, group_f[it, 0])
            for j in range(1, n_g - 1):
                @pl.when(group > j)
                def _():
                    link[...] = group_f[it, j] + row_times(link[0:1, :], p_ref.at[j - 1])

        entered = link[0:1, :]
        column = to_column(entered)
        t_b = column_times(column, t_ref.at[0]) + f_a
        back_b = b_b - row_times(t_b, e_ref.at[1])
        back_a = b_a - column_times(column, e_ref.at[0])
        group_b[it, group] = broad(back_a + row_times_t(back_b, t_ref.at[0]))
        for i in range(1, n_g):
            group_copy(group_b, b_send, b_recv, i).start()

        zero_back()
        column = to_column(pick_odd(t_b, entered))
        fixed = update[...] - jnp.concatenate([column_times(column, q_ref.at[k]) for k in range(count)], axis=0)

        @pl.when(first)
        def _():
            far_arrive(lambda source: group < source)
            pass_arrive(lambda source: group < source)

        for i in range(1, n_g):
            group_copy(group_b, b_send, b_recv, i).wait()

        link[...] = jnp.where(group == n_g - 1, 0.0, group_b[it, n_g - 1])
        for j in reversed(range(1, n_g - 1)):
            @pl.when(group < j)
            def _():
                link[...] = group_b[it, j] + row_times_t(link[0:1, :], p_ref.at[j - 1])

        entered = link[0:1, :]
        later = pick_odd(entered, back_b + row_times_t(entered, t_ref.at[1]))
        column = to_column(later)
        fixed = fixed + jnp.concatenate([column_times(column, x_ref.at[k]) for k in range(count)], axis=0)
        own[it + 1] = own[it] - fixed
        share_camera(it + 1)

        @pl.when(first)
        def _():
            @pl.when(group < n_g - 1)
            def _():
                ring_copy().wait_send()

            far_arrive(lambda source: group > source)
            pass_arrive(lambda source: group > source)

            @pl.when(inner_group)
            def _():
                far_each(lambda to: to >= 0, lambda copy: copy.wait_send())

        await_cameras(it + 1)
        return carry

    lax.fori_loop(0, ITERS, inner_step, 0)
    cam_out[...] = own[ITERS]
    cameras = every[ITERS].reshape(n_c * count, width)
    eliminate_points(
        False, cameras, pick, pick_t, cj_ref, pj_ref, res_ref,
        jnp.concatenate([high_damp] * 2, axis=1), point_out, seen, parts,
    )


def paired_shards(n_c, n_p, cam_jac, point_jac, residual, obs_cam, damp_exp, cam_step, diag_inverse, coupling):
    blocks, observers = obs_cam.shape
    count, width = cam_step.shape
    total_blocks = count * n_c
    pairs = observers // 2
    rows = pairs * blocks
    n_g = n_c // 2
    cj, pj, obs = cam_jac.transpose(1, 0, 2), point_jac.transpose(1, 0, 2), obs_cam.T
    res = residual.reshape(blocks, 2, pairs, 128).transpose(0, 2, 1, 3).reshape(2 * rows, 128)
    sem = pltpu.SemaphoreType.DMA

    def vmem(*shape, dtype=F32):
        return pltpu.VMEM(shape, dtype)

    camera, out = pl.pallas_call(
        functools.partial(paired_kernel, n_c, n_p),
        in_specs=[ANY] * 8,
        out_specs=[VMEM, VMEM],
        out_shape=[
            jax.ShapeDtypeStruct((count, width), F32),
            jax.ShapeDtypeStruct((3, blocks, 64), F32),
        ],
        scratch_shapes=[pltpu.VMEM(x.shape, x.dtype) for x in (obs, damp_exp, cj, pj, res, diag_inverse, coupling)]
        + [
            vmem(count, width // 2, width),
            vmem(count, width, width),
            vmem(count, width, width),
            vmem(2, width, width),
            vmem(2, width, width),
            vmem(n_g - 2, width, width),
            vmem(width // 2, width),
            vmem(2 * rows, 3 * total_blocks, dtype=BF16),
            vmem(total_blocks, 2 * rows, dtype=BF16),
            vmem(2 * rows, width),
            vmem(2, 2 * rows, width, dtype=BF16),
            vmem(total_blocks, width),
            vmem(ITERS + 1, count, width),
            vmem(ITERS + 1, n_c, count, width),
            vmem(ITERS, n_c, count, width),
            vmem(ITERS, n_p, count + 8, width),
            vmem(ITERS, n_p, 8, width),
            vmem(count, width),
            vmem(count, width),
            vmem(ITERS, n_g, 8, width),
            vmem(ITERS, n_g, 8, width),
            vmem(8, width),
            vmem(8, width),
            vmem(8, width),
            sem((6,)), sem((2, count)), sem((ITERS + 1, n_c)), sem((ITERS + 1, n_c)), sem((ITERS, n_c)), sem((ITERS, n_c)),
            sem((ITERS, n_p)), sem((ITERS, n_p)), sem((ITERS, n_p)), sem((ITERS, n_p)),
            sem((ITERS, n_g)), sem((ITERS, n_g)), sem((ITERS, n_g)), sem((ITERS, n_g)),
            sem((count,)), sem((count,)), sem((count,)), sem((count,)),
            sem((2,)), sem((2,)), sem((4,)), sem((4,)),
            sem((n_g,)), sem((n_g - 2,)), sem((n_g - 2,)), sem((n_g - 2,)), sem(()), sem(()),
        ],
        compiler_params=pltpu.CompilerParams(
            collective_id=0, has_side_effects=True, vmem_limit_bytes=60 << 20
        ),
        name="camera_steps",
    )(obs, damp_exp, cam_step, cj, pj, res, diag_inverse, coupling)
    return camera, out.transpose(1, 0, 2)


def solution(mesh):
    in_specs = (
        P(("chain", "pts"), None, None),
        P(("chain", "pts"), None, None),
        P(("chain", "pts"), None, None),
        P(("chain", "pts"), None),
        P(),
        P("chain", None),
        P("chain", None, None),
        P("chain", None, None),
    )
    out_specs = (P("chain", None), P(("chain", "pts"), None, None))
    n_c, n_p = mesh.shape["chain"], mesh.shape["pts"]
    paired = n_c % 2 == 0 and 6 <= n_c <= 16 and n_p % 2 == 0
    inner = functools.partial(paired_shards if paired else shards, n_c, n_p)
    return jax.shard_map(inner, mesh=mesh, in_specs=in_specs, out_specs=out_specs, check_vma=False)
```

```python
import functools

import jax
import jax.numpy as jnp
from jax import lax
from jax.experimental import pallas as pl
from jax.experimental.pallas import tpu as pltpu
from jax.sharding import PartitionSpec as P

ITERS = 2
MESH = pl.DeviceIdType.MESH
F32, BF16 = jnp.float32, jnp.bfloat16
VMEM = pl.BlockSpec(memory_space=pltpu.VMEM)
ANY = pl.BlockSpec(memory_space=pl.ANY)


def dot_rows(x, panel):
    return lax.dot_general(x, panel, (((1,), (0,)), ((), ())), preferred_element_type=F32)


def dot_cols(x, panel):
    return lax.dot_general(x, panel, (((1,), (1,)), ((), ())), preferred_element_type=F32)


def halves(x):
    high = x.astype(BF16)
    return high, (x - high.astype(F32)).astype(BF16)


def thirds(x):
    high = x.astype(BF16)
    rest = x - high.astype(F32)
    mid = rest.astype(BF16)
    return high, mid, (rest - mid.astype(F32)).astype(BF16)


def eliminate(adjoint_out, cameras, pick_ref, pick_t_ref, cj_ref, pj_ref, res_ref, damp, out_ref, seen, parts):
    rows = res_ref.shape[1]
    blocks = rows // 4
    high, mid, low = thirds(cameras)
    pick = pick_ref[...]
    seen[...] = (dot_rows(pick, low) + dot_rows(pick, mid)) + dot_rows(pick, high)
    step = 16
    left = lax.broadcasted_iota(jnp.int32, (step, 128), 1) < 64

    def swap(x):
        return pltpu.roll(x, 64, 1)

    def chunk(i, carry):
        at = pl.multiple_of(i * step, step)
        misfits, points = [], []
        hess = [None] * 6
        target = [None] * 3
        pairs = ((0, 0), (0, 1), (0, 2), (1, 1), (1, 2), (2, 2))
        for tp in range(4):
            here = pl.ds(tp * blocks + at, step)
            there = pl.ds(rows + tp * blocks + at, step)
            cams = []
            for c in range(3):
                even = seen[here, c * 128 : (c + 1) * 128]
                odd = seen[there, c * 128 : (c + 1) * 128]
                cams.append(jnp.where(left, even, swap(odd)))
                cams.append(jnp.where(left, swap(even), odd))
            for a in range(2):
                miss = res_ref[a, here, :]
                for m in range(6):
                    miss = miss + cj_ref[6 * a + m, here, :].astype(F32) * cams[m]
                terms = [pj_ref[3 * a + n, here, :].astype(F32) for n in range(3)]
                misfits.append(miss)
                points.append(terms)
                for e, (n, k) in enumerate(pairs):
                    new = terms[n] * terms[k]
                    hess[e] = new if hess[e] is None else hess[e] + new
                for n in range(3):
                    new = terms[n] * miss
                    target[n] = new if target[n] is None else target[n] + new
        hess = [h + swap(h) for h in hess]
        ta, tb, tc = [t + swap(t) for t in target]
        aa, ab, ac, bb, bc, cc = hess
        aa, bb, cc = aa + damp, bb + damp, cc + damp
        cof_aa = bb * cc - bc * bc
        cof_ab = ac * bc - ab * cc
        cof_ac = ab * bc - ac * bb
        cof_bb = aa * cc - ac * ac
        cof_bc = ab * ac - aa * bc
        cof_cc = aa * bb - ab * ab
        det = aa * cof_aa + ab * cof_ab + ac * cof_ac
        sol = (
            (cof_aa * ta + cof_ab * tb + cof_ac * tc) / det,
            (cof_ab * ta + cof_bb * tb + cof_bc * tc) / det,
            (cof_ac * ta + cof_bc * tb + cof_cc * tc) / det,
        )
        if not adjoint_out:
            for n in range(3):
                out_ref[n, pl.ds(at, step), :] = -sol[n]
            return carry
        for tp in range(4):
            here = pl.ds(tp * blocks + at, step)
            there = pl.ds(rows + tp * blocks + at, step)
            left_over = []
            for a in range(2):
                terms = points[2 * tp + a]
                left_over.append(
                    misfits[2 * tp + a]
                    - (terms[0] * sol[0] + terms[1] * sol[1] + terms[2] * sol[2])
                )
            adj = [
                cj_ref[m, here, :].astype(F32) * left_over[0]
                + cj_ref[6 + m, here, :].astype(F32) * left_over[1]
                for m in range(6)
            ]
            for c in range(3):
                span = slice(c * 128, (c + 1) * 128)
                even = jnp.where(left, adj[2 * c], swap(adj[2 * c + 1]))
                odd = jnp.where(left, swap(adj[2 * c]), adj[2 * c + 1])
                for part, value in enumerate(thirds(even)):
                    parts[part, here, span] = value
                for part, value in enumerate(thirds(odd)):
                    parts[part, there, span] = value
        return carry

    lax.fori_loop(0, blocks // step, chunk, 0)
    if adjoint_out:
        pick_t = pick_t_ref[...]
        out_ref[...] = (
            dot_rows(pick_t, parts[2]) + dot_rows(pick_t, parts[1])
        ) + dot_rows(pick_t, parts[0])


def split_row(v):
    row = lax.broadcasted_iota(jnp.int32, v.shape, 0)
    high = v.astype(BF16).astype(F32)
    rest = v - high
    mid = rest.astype(BF16).astype(F32)
    low = rest - mid
    return jnp.where(row == 0, high, jnp.where(row == 1, mid, jnp.where(row == 2, low, 0.0))).astype(BF16)


def total(y):
    return jnp.broadcast_to(jnp.sum(y, axis=0, keepdims=True), y.shape)


def times(v, panel):
    return total(dot_rows(split_row(v), panel))


def times_t(v, panel):
    return total(dot_cols(split_row(v), panel))


def stacked(dot, x, panel):
    rows = x.shape[0]
    both = dot(jnp.concatenate(halves(x), axis=0), panel)
    return both[:rows] + both[rows:]


def whole_kernel(
    n_c, n_p,
    order_ref, cam_ref, damp_ref, cj_hbm, pj_hbm, res_hbm, d_hbm, c_hbm,
    cam_out, point_out,
    cj_ref, pj_ref, res_ref, d_ref, c_ref, wh_ref, wl_ref, xh_ref, xl_ref, rh_ref, rl_ref, run_f, run_b,
    pick, pick_t, seen, parts, dense, own, every,
    landed, piece, grad, solved, update, carry_in, carry_out, first_in, first_out, entry,
    run_nb, nh_ref, nl_ref, ph_ref, pk_ref,
    load_sem, rs_send, rs_recv, pts_send, pts_recv, ring_send, ring_recv, first_send, first_recv, all_send, all_recv, nb_send, nb_recv,
):
    me_c, me_p = lax.axis_index("chain"), lax.axis_index("pts")
    count, width = cam_ref.shape
    rows = res_ref.shape[1]
    loads = [
        pltpu.make_async_copy(src, dst, load_sem.at[i])
        for i, (src, dst) in enumerate(
            ((d_hbm, d_ref), (c_hbm, c_ref), (cj_hbm, cj_ref), (pj_hbm, pj_ref), (res_hbm, res_ref))
        )
    ]
    for load in loads:
        load.start()

    barrier = pltpu.get_barrier_semaphore()

    @pl.loop(1, n_c)
    def _(i):
        pl.semaphore_signal(
            barrier, inc=1, device_id=(lax.rem(me_c + i, n_c), me_p), device_id_type=MESH
        )

    for i in range(1, n_p):
        pl.semaphore_signal(
            barrier, inc=1, device_id=(me_c, lax.rem(me_p + i, n_p)), device_id_type=MESH
        )
    pl.semaphore_wait(barrier, n_c + n_p - 2)

    def all_copy(turn, i):
        return pltpu.make_async_remote_copy(
            src_ref=own.at[turn],
            dst_ref=every.at[turn, me_c],
            send_sem=all_send.at[turn, i],
            recv_sem=all_recv.at[turn, i],
            device_id=(lax.rem(me_c + i, n_c), me_p),
            device_id_type=MESH,
        )

    def share_camera(turn):
        @pl.loop(1, n_c)
        def _(i):
            all_copy(turn, i).start()

        every[turn, me_c] = own[turn]

    def await_cameras(turn):
        @pl.loop(1, n_c)
        def _(i):
            all_copy(turn, i).wait()

    own[0] = cam_ref[...]
    share_camera(0)

    cams = lax.broadcasted_iota(jnp.int32, pick_t.shape, 0)
    chosen = jnp.where(cams == jnp.broadcast_to(order_ref[...], pick_t.shape), 1.0, 0.0)
    pick_t[...] = chosen.astype(BF16)
    pick[...] = chosen.T.astype(BF16)

    unit = (
        lax.broadcasted_iota(jnp.int32, (width, width), 0)
        == lax.broadcasted_iota(jnp.int32, (width, width), 1)
    ).astype(F32)
    run_f[...] = unit
    run_b[...] = unit

    def map_ahead(k, carry):
        made = -stacked(dot_rows, run_f[...], d_ref[k])
        high, low = halves(made)
        wh_ref[k] = high
        wl_ref[k] = low
        run_f[...] = stacked(dot_rows, made, c_ref[k])
        return carry

    def map_back(i, carry):
        k = count - 1 - i
        made = stacked(dot_cols, -stacked(dot_cols, run_b[...], c_ref[k]), d_ref[k])
        run_b[...] = made
        high, low = halves(made)
        xh_ref[k] = high
        xl_ref[k] = low
        return carry

    odd = lax.rem(me_c, 2)
    swap_maps = pltpu.make_async_remote_copy(
        src_ref=run_f, dst_ref=run_nb, send_sem=nb_send, recv_sem=nb_recv,
        device_id=(me_c + 1 - 2 * odd, me_p), device_id_type=MESH,
    )

    def pair_map():
        high, low = halves(run_f[...])
        rh_ref[...] = high
        rl_ref[...] = low
        swap_maps.wait()
        mine, other = run_f[...], run_nb[...]
        nh_ref[...], nl_ref[...] = halves(other)
        early = jnp.where(odd == 1, other, mine)
        late_high, late_low = halves(jnp.where(odd == 1, mine, other))
        high, low = halves(stacked(dot_rows, early, late_high) + stacked(dot_rows, early, late_low))
        ph_ref[...] = high
        pk_ref[...] = low

    loads[0].wait()
    loads[1].wait()
    lax.fori_loop(0, count, map_ahead, 0)
    swap_maps.start()
    for load in loads[2:]:
        load.wait()
    await_cameras(0)

    def zero_ahead():
        carried = None
        for k in range(count):
            g = jnp.broadcast_to(grad[k : k + 1, :], carry_in.shape[2:])
            s = times(g if carried is None else g - carried, d_ref[k])
            solved[k : k + 1, :] = s[0:1]
            if k < count - 1:
                carried = times(s, c_ref[k])

    def zero_back():
        later = None
        for k in reversed(range(count)):
            r = jnp.broadcast_to(solved[k : k + 1, :], carry_in.shape[2:])
            if later is not None:
                r = r - times_t(later, c_ref[k])
            later = times_t(r, d_ref[k])
            update[k : k + 1, :] = later[0:1]

    def reach(vectors, high_ref, low_ref):
        acc = None
        for k in range(count):
            x = split_row(jnp.broadcast_to(vectors[k : k + 1, :], carry_in.shape[2:]))
            new = dot_cols(x, high_ref[k]) + dot_cols(x, low_ref[k])
            acc = new if acc is None else acc + new
        return -total(acc)

    def correct(x, out, high_ref, low_ref):
        for k in range(count):
            y = dot_rows(x, high_ref[k]) + dot_rows(x, low_ref[k])
            out[k : k + 1, :] = out[k : k + 1, :] + jnp.sum(y, axis=0, keepdims=True)

    def inner_step(it, carry):
        damp = damp_ref[it]
        cameras = every[it].reshape(n_c * count, width)
        eliminate(True, cameras, pick, pick_t, cj_ref, pj_ref, res_ref, damp[:, :128], dense, seen, parts)

        def rs_copy(i):
            to = lax.rem(me_c + i, n_c)
            return pltpu.make_async_remote_copy(
                src_ref=dense.at[pl.ds(pl.multiple_of(to * count, count), count)],
                dst_ref=landed.at[it, i],
                send_sem=rs_send.at[it, i],
                recv_sem=rs_recv.at[it, i],
                device_id=(to, me_p),
                device_id_type=MESH,
            )

        @pl.loop(1, n_c)
        def _(i):
            rs_copy(i).start()

        landed[it, 0] = dense[pl.ds(pl.multiple_of(me_c * count, count), count), :]

        @pl.when(it == 0)
        def _():
            lax.fori_loop(0, count, map_back, 0)

        @pl.loop(1, n_c)
        def _(i):
            rs_copy(i).wait()

        mine = jnp.sum(landed[it], axis=0)

        def pts_copy(i):
            return pltpu.make_async_remote_copy(
                src_ref=piece.at[it, me_p],
                dst_ref=piece.at[it, me_p],
                send_sem=pts_send.at[it, i],
                recv_sem=pts_recv.at[it, i],
                device_id=(me_c, lax.rem(me_p + i, n_p)),
                device_id_type=MESH,
            )

        piece[it, me_p] = mine
        for i in range(1, n_p):
            pts_copy(i).start()

        @pl.when(it == 0)
        def _():
            pair_map()

        for i in range(1, n_p):
            pts_copy(i).wait()
        grad[...] = jnp.sum(piece[it], axis=0) + damp * own[it]

        def hand(way):
            return pltpu.make_async_remote_copy(
                src_ref=first_out.at[it, way], dst_ref=first_in.at[it, way],
                send_sem=first_send.at[it, way], recv_sem=first_recv.at[it, way],
                device_id=(me_c + 1 - 2 * odd, me_p), device_id_type=MESH,
            )

        def ring(way, far):
            to = lax.rem(me_c + (n_c - far if way else far), n_c)
            return pltpu.make_async_remote_copy(
                src_ref=carry_out.at[it, way], dst_ref=carry_in.at[it, way],
                send_sem=ring_send.at[it, way, far - 1], recv_sem=ring_recv.at[it, way],
                device_id=(to, me_p), device_id_type=MESH,
            )

        def seat(way):
            turn = n_c - 1 - me_c if way else me_c
            return lax.rem(turn, 2) == 1, turn // 2

        def pass_on(way, reached, map_high, map_low, sweep):
            second, group = seat(way)
            dot = dot_cols if way else dot_rows

            def arrive():
                @pl.when(group == 0)
                def _():
                    carry_in[it, way] = jnp.zeros(carry_in.shape[2:], F32)

                @pl.when(group > 0)
                def _():
                    ring(way, 2).wait_recv()

                return carry_in[it, way]

            first_out[it, way] = reached

            @pl.when(jnp.logical_not(second))
            def _():
                hand(way).start()
                sweep()
                entry[...] = arrive()

            @pl.when(second)
            def _():
                @pl.when(group >= 2)
                def _():
                    sweep()

                hand(way).wait_recv()
                given = first_in[it, way]
                x = split_row(given)
                both = first_out[it, way] + total(dot_rows(x, map_high[...]) + dot_rows(x, map_low[...]))
                x = split_row(arrive())
                carry_out[it, way] = both + total(dot(x, ph_ref[...]) + dot(x, pk_ref[...]))

                @pl.when(group < n_c // 2 - 1)
                def _():
                    ring(way, 2).start()
                    ring(way, 1).start()

                entry[...] = given + total(dot(x, nh_ref[...]) + dot(x, nl_ref[...]))

                @pl.when(group < 2)
                def _():
                    sweep()

            return split_row(entry[...])

        def drain(way):
            second, group = seat(way)

            @pl.when(jnp.logical_not(second))
            def _():
                hand(way).wait_send()

            @pl.when(jnp.logical_and(second, group < n_c // 2 - 1))
            def _():
                ring(way, 2).wait_send()
                ring(way, 1).wait_send()

        x = pass_on(0, reach(grad, xh_ref, xl_ref), rh_ref, rl_ref, zero_ahead)
        correct(x, solved, wh_ref, wl_ref)
        x = pass_on(1, reach(solved, wh_ref, wl_ref), xh_ref.at[0], xl_ref.at[0], zero_back)
        correct(x, update, xh_ref, xl_ref)
        own[it + 1] = own[it] - update[...]
        share_camera(it + 1)

        drain(0)
        drain(1)
        await_cameras(it + 1)
        return carry

    lax.fori_loop(0, ITERS, inner_step, 0)
    cam_out[...] = own[ITERS]
    cameras = every[ITERS].reshape(n_c * count, width)
    eliminate(
        False, cameras, pick, pick_t, cj_ref, pj_ref, res_ref, damp_ref[ITERS - 1][:, :128], point_out, seen, parts
    )


def shards(n_c, n_p, cam_jac, point_jac, residual, obs_cam, damp_exp, cam_step, diag_inverse, coupling):
    blocks, observers = obs_cam.shape
    count, width = cam_step.shape
    total_blocks = count * n_c
    pairs = observers // 2
    rows = pairs * blocks

    def by_pair(x):
        comps = x.shape[1]
        return x.reshape(blocks, comps, pairs, 128).transpose(1, 2, 0, 3).reshape(comps, rows, 128)

    cj, pj, res = by_pair(cam_jac), by_pair(point_jac), by_pair(residual)
    order = obs_cam.reshape(blocks, pairs, 2).transpose(2, 1, 0).reshape(1, -1)
    wide = jnp.tile(jnp.exp2(damp_exp.astype(F32)), (1, 6))[:, None, :]
    panel = pltpu.VMEM((count, width, width), BF16)
    square = (width, width)
    sem = pltpu.SemaphoreType.DMA
    camera, out = pl.pallas_call(
        functools.partial(whole_kernel, n_c, n_p),
        in_specs=[VMEM] * 3 + [ANY] * 5,
        out_specs=[VMEM, VMEM],
        out_shape=[
            jax.ShapeDtypeStruct((count, width), F32),
            jax.ShapeDtypeStruct((3, blocks, 128), F32),
        ],
        scratch_shapes=[pltpu.VMEM(x.shape, x.dtype) for x in (cj, pj, res)]
        + [panel] * 6
        + [pltpu.VMEM(square, BF16)] * 2
        + [pltpu.VMEM(square, F32)] * 2
        + [
            pltpu.VMEM((2 * rows, total_blocks), BF16),
            pltpu.VMEM((total_blocks, 2 * rows), BF16),
            pltpu.VMEM((2 * rows, width), F32),
            pltpu.VMEM((3, 2 * rows, width), BF16),
            pltpu.VMEM((total_blocks, width), F32),
            pltpu.VMEM((ITERS + 1, count, width), F32),
            pltpu.VMEM((ITERS + 1, n_c, count, width), F32),
            pltpu.VMEM((ITERS, n_c, count, width), F32),
            pltpu.VMEM((ITERS, n_p, count, width), F32),
            pltpu.VMEM((count, width), F32),
            pltpu.VMEM((count, width), F32),
            pltpu.VMEM((count, width), F32),
            pltpu.VMEM((ITERS, 2, 8, width), F32),
            pltpu.VMEM((ITERS, 2, 8, width), F32),
            pltpu.VMEM((ITERS, 2, 8, width), F32),
            pltpu.VMEM((ITERS, 2, 8, width), F32),
            pltpu.VMEM((8, width), F32),
            pltpu.VMEM(square, F32),
            pltpu.VMEM(square, BF16),
            pltpu.VMEM(square, BF16),
            pltpu.VMEM(square, BF16),
            pltpu.VMEM(square, BF16),
            sem((5,)), sem((ITERS, n_c)), sem((ITERS, n_c)), sem((ITERS, n_p)), sem((ITERS, n_p)),
            sem((ITERS, 2, 2)), sem((ITERS, 2)), sem((ITERS, 2)), sem((ITERS, 2)),
            sem((ITERS + 1, n_c)), sem((ITERS + 1, n_c)), sem(()), sem(()),
        ],
        compiler_params=pltpu.CompilerParams(
            collective_id=0, has_side_effects=True, vmem_limit_bytes=48 << 20
        ),
        name="camera_steps",
    )(order, cam_step, wide, cj, pj, res, diag_inverse, coupling)
    return camera, out[:, :, :64].transpose(1, 0, 2)


def lanes(x, c):
    return x[:, c * 128 : (c + 1) * 128]


def to_column(x):
    return jnp.concatenate(
        [jnp.broadcast_to(lanes(x, c), (128, 128)).T for c in range(x.shape[1] // 128)], axis=0
    )


def column_times(column, m):
    return jnp.concatenate(
        [jnp.sum(m[:, c * 128 : (c + 1) * 128] * column, axis=0, keepdims=True) for c in range(m.shape[1] // 128)],
        axis=1,
    )


def spread(x, m):
    acc = None
    for c in range(m.shape[1] // 128):
        new = m[:, c * 128 : (c + 1) * 128] * lanes(x, c)
        acc = new if acc is None else acc + new
    return acc


def lane_sum(acc):
    parts = jnp.concatenate(thirds(acc), axis=1)
    return dot_cols(jnp.ones((8, parts.shape[1]), BF16), parts)[0:1]


def row_times(x, m):
    return column_times(to_column(x), m)


def row_times_t(x, m):
    return lane_sum(spread(x, m))


def eliminate_points(adjoint_out, cameras, pick_ref, pick_t_ref, cj_ref, pj_ref, res_ref, damp, out_ref, seen, parts):
    blocks = cj_ref.shape[1]
    pairs = cj_ref.shape[2] // 128
    rows = pairs * blocks
    seen[...] = dot_rows(pick_ref[...], jnp.concatenate(thirds(cameras), axis=0))
    step = 16
    left = lax.broadcasted_iota(jnp.int32, (step, 128), 1) < 64

    def swap(x):
        return pltpu.roll(x, 64, 1)

    def chunk(i, carry):
        at = pl.multiple_of(i * step, step)
        body = pl.ds(at, step)
        misfits, points = [], []
        hess = [None] * 6
        target = [None] * 3
        order = ((0, 0), (0, 1), (0, 2), (1, 1), (1, 2), (2, 2))
        for tp in range(pairs):
            here = pl.ds(tp * blocks + at, step)
            there = pl.ds(rows + tp * blocks + at, step)
            span = slice(tp * 128, (tp + 1) * 128)
            cams = []
            for c in range(3):
                even = seen[here, c * 128 : (c + 1) * 128]
                odd = seen[there, c * 128 : (c + 1) * 128]
                cams.append(jnp.where(left, even, swap(odd)))
                cams.append(jnp.where(left, swap(even), odd))
            for a in range(2):
                miss = res_ref[pl.ds(at * 2 * pairs + tp * 2 + a, step, stride=2 * pairs), :]
                for m in range(6):
                    miss = miss + cj_ref[6 * a + m, body, span].astype(F32) * cams[m]
                terms = [pj_ref[3 * a + n, body, span].astype(F32) for n in range(3)]
                misfits.append(miss)
                points.append(terms)
                for e, (n, k) in enumerate(order):
                    new = terms[n] * terms[k]
                    hess[e] = new if hess[e] is None else hess[e] + new
                for n in range(3):
                    new = terms[n] * miss
                    target[n] = new if target[n] is None else target[n] + new
        hess = [h + swap(h) for h in hess]
        ta, tb, tc = [t + swap(t) for t in target]
        aa, ab, ac, bb, bc, cc = hess
        aa, bb, cc = aa + damp, bb + damp, cc + damp
        cof_aa = bb * cc - bc * bc
        cof_ab = ac * bc - ab * cc
        cof_ac = ab * bc - ac * bb
        cof_bb = aa * cc - ac * ac
        cof_bc = ab * ac - aa * bc
        cof_cc = aa * bb - ab * ab
        det = aa * cof_aa + ab * cof_ab + ac * cof_ac
        sol = (
            (cof_aa * ta + cof_ab * tb + cof_ac * tc) / det,
            (cof_ab * ta + cof_bb * tb + cof_bc * tc) / det,
            (cof_ac * ta + cof_bc * tb + cof_cc * tc) / det,
        )
        if not adjoint_out:
            for n in range(3):
                out_ref[n, body, :] = -sol[n][:, : out_ref.shape[2]]
            return carry
        for tp in range(pairs):
            here = pl.ds(tp * blocks + at, step)
            there = pl.ds(rows + tp * blocks + at, step)
            span = slice(tp * 128, (tp + 1) * 128)
            left_over = []
            for a in range(2):
                terms = points[2 * tp + a]
                left_over.append(
                    misfits[2 * tp + a]
                    - (terms[0] * sol[0] + terms[1] * sol[1] + terms[2] * sol[2])
                )
            adj = [
                cj_ref[m, body, span].astype(F32) * left_over[0]
                + cj_ref[6 + m, body, span].astype(F32) * left_over[1]
                for m in range(6)
            ]
            for c in range(3):
                out = slice(c * 128, (c + 1) * 128)
                even = jnp.where(left, adj[2 * c], swap(adj[2 * c + 1]))
                odd = jnp.where(left, swap(adj[2 * c]), adj[2 * c + 1])
                for part, value in enumerate(halves(even)):
                    parts[part, here, out] = value
                for part, value in enumerate(halves(odd)):
                    parts[part, there, out] = value
        return carry

    lax.fori_loop(0, blocks // step, chunk, 0)
    if adjoint_out:
        pick_t = pick_t_ref[...]
        out_ref[...] = dot_rows(pick_t, parts[1]) + dot_rows(pick_t, parts[0])


def paired_kernel(
    n_c, n_p,
    obs_hbm, exp_hbm, cam_hbm, cj_hbm, pj_hbm, res_hbm, d_hbm, c_hbm,
    cam_out, point_out,
    obs_ref, exp_ref, cj_ref, pj_ref, res_ref, d_ref, c_ref,
    w_ref, m_ref, t_ref, e_ref, p_ref, run, runs,
    pick, pick_t, seen, parts, dense, own, every, landed, piece, told, near,
    solved, update, group_f, group_b, ring_out, ring_in, link,
    load_sem, panel_sem, all_send, all_recv, rs_send, rs_recv, pts_send, pts_recv, told_send, told_recv,
    near_send, near_recv, f_send, f_recv, b_send, b_recv, m_send, m_recv,
    pair_send, pair_recv, core_send, core_recv, far_send, far_recv, pass_send, pass_recv, ring_send, ring_recv,
):
    me_c, me_p = lax.axis_index("chain"), lax.axis_index("pts")
    n_g = n_c // 2
    group, odd = me_c // 2, lax.rem(me_c, 2)
    beside = me_c + 1 - 2 * odd
    twin = me_p + 1 - 2 * lax.rem(me_p, 2)
    count, width = cam_hbm.shape
    half = width // 2
    steps = 2

    def apart(i):
        to, bit = 0, 1
        while bit < n_c:
            mine = lax.rem(me_c // bit, 2)
            to = to + bit * (1 - mine if i & bit else mine)
            bit = 2 * bit
        return to

    def settle(ref, *sems):
        for sem in sems:
            pltpu.make_async_copy(ref, ref, sem).wait()
    mine_rows = pl.ds(pl.multiple_of(lax.rem(me_p, 2) * half, 8), half)

    barrier = pltpu.get_barrier_semaphore()

    for i in range(1, n_c):
        pl.semaphore_signal(
            barrier, inc=1, device_id=(lax.rem(me_c + i, n_c), me_p), device_id_type=MESH
        )
    for i in range(1, n_p):
        to = lax.rem(me_p + i, n_p)
        pl.semaphore_signal(barrier, inc=1, device_id=(me_c, to), device_id_type=MESH)
        pl.semaphore_signal(barrier, inc=1, device_id=(beside, to), device_id_type=MESH)

    loads = [
        pltpu.make_async_copy(src, dst, load_sem.at[i])
        for i, (src, dst) in enumerate(
            (
                (cam_hbm, own.at[0]), (obs_hbm, obs_ref), (exp_hbm, exp_ref),
                (cj_hbm, cj_ref), (pj_hbm, pj_ref), (res_hbm, res_ref),
            )
        )
    ]

    def panel_load(k):
        at = pl.ds(k * steps, steps)
        return (
            pltpu.make_async_copy(d_hbm.at[at], d_ref.at[at], panel_sem.at[0, k]),
            pltpu.make_async_copy(c_hbm.at[at], c_ref.at[at], panel_sem.at[1, k]),
        )

    for k in range(count // steps):
        for load in panel_load(k):
            load.start()
        if k == 0:
            for load in loads[:3]:
                load.start()
    for load in loads[3:]:
        load.start()

    def remote(src, dst, send, recv, chain, pts):
        return pltpu.make_async_remote_copy(
            src_ref=src, dst_ref=dst, send_sem=send, recv_sem=recv,
            device_id=(chain, pts), device_id_type=MESH,
        )

    def share_camera(turn):
        for i in reversed(range(1, n_c)):
            remote(
                own.at[turn], every.at[turn, me_c], all_send.at[turn], all_recv.at[turn], apart(i), me_p
            ).start()
        every[turn, me_c] = own[turn]

    def await_cameras(turn):
        settle(every.at[turn, pl.ds(0, n_c - 1)], all_send.at[turn], all_recv.at[turn])

    def map_copy(k):
        part = m_ref.at[k, :, mine_rows]
        return remote(part, part, m_send, m_recv, me_c, twin)

    def pair_copy(ref, i):
        return remote(ref.at[odd, mine_rows], ref.at[odd, mine_rows], pair_send.at[i], pair_recv.at[i], beside, me_p)

    def core_copy(ref, seat, i):
        return remote(ref.at[seat, mine_rows], ref.at[seat, mine_rows], core_send.at[i], core_recv.at[i], me_c, twin)

    own_slot = jnp.clip(group - 1, 0, n_g - 3)

    def far_each(where, act):
        for i in range(1, n_g):
            to = lax.rem(group + i, n_g)

            @pl.when(where(to))
            def _():
                act(
                    remote(
                        p_ref.at[own_slot, mine_rows], p_ref.at[own_slot, mine_rows],
                        far_send.at[i], far_recv.at[own_slot], 2 * to + odd, me_p,
                    )
                )

    def far_arrive(where):
        for slot in range(n_g - 2):
            @pl.when(where(slot + 1))
            def _():
                remote(
                    p_ref.at[slot, mine_rows], p_ref.at[slot, mine_rows], far_send.at[0], far_recv.at[slot],
                    beside, me_p,
                ).wait_recv()
                pass_copy(slot).start()

    def pass_arrive(where):
        for slot in range(n_g - 2):
            @pl.when(where(slot + 1))
            def _():
                pass_copy(slot).wait()

    def pass_copy(slot):
        return remote(
            p_ref.at[slot, mine_rows], p_ref.at[slot, mine_rows], pass_send.at[slot], pass_recv.at[slot], me_c, twin
        )

    unit_rows = (
        lax.broadcasted_iota(jnp.int32, (half, width), 0) + lax.rem(me_p, 2) * half
        == lax.broadcasted_iota(jnp.int32, (half, width), 1)
    ).astype(F32)
    run[...] = unit_rows

    runs[0:half] = jnp.zeros((half, width), F32)
    runs[half:] = unit_rows

    def map_ahead(i, carry):
        for load in panel_load(i):
            load.wait()
        held = run[...]
        for u in range(steps):
            k = i * steps + u
            made = -stacked(dot_rows, held, d_ref[k])
            w_ref[k] = made
            held = stacked(dot_rows, made, c_ref[k])
        run[...] = held
        return carry

    def map_back(i, carry):
        held = runs[...]
        for u in range(steps):
            k = count - 1 - i * steps - u
            held = stacked(dot_cols, held, c_ref[k])
            held = -jnp.concatenate([held[:half] + w_ref[k], held[half:]], axis=0)
            held = stacked(dot_cols, held, d_ref[k])
            m_ref[k, 0, mine_rows] = held[:half]
            m_ref[k, 1, mine_rows] = held[half:]
            map_copy(k).start()
        runs[...] = held
        return carry

    lax.fori_loop(0, 1, map_ahead, 0)

    for load in loads[:3]:
        load.wait()
    obs = obs_ref[...]
    observers = obs.shape[0]
    order = jnp.concatenate(
        [obs[t : t + 1, :] for h in range(2) for t in range(h, observers, 2)], axis=1
    )
    cams = lax.broadcasted_iota(jnp.int32, pick_t.shape, 0)
    chosen = jnp.where(cams == jnp.broadcast_to(order, pick_t.shape), 1.0, 0.0)
    pick_t[...] = chosen.astype(BF16)
    pick[...] = jnp.concatenate([chosen] * 3, axis=0).T.astype(BF16)
    damps = jnp.exp2(exp_ref[...].astype(F32))
    low_damp, high_damp = damps[0:1], damps[ITERS - 1 : ITERS]

    pl.semaphore_wait(barrier, n_c - 1 + 2 * (n_p - 1))

    share_camera(0)
    lax.fori_loop(1, count // steps, map_ahead, 0)
    t_ref[odd, mine_rows] = run[...]
    pair_copy(t_ref, 0).start()
    core_copy(t_ref, odd, 0).start()
    lax.fori_loop(0, 1, map_back, 0)
    for load in loads[3:]:
        load.wait()
    await_cameras(0)

    inner_group = jnp.logical_and(group >= 1, group <= n_g - 2)

    def broad(row):
        return jnp.broadcast_to(row, (8, width))

    def zero_ahead(grad):
        carried = None
        for k in range(count):
            g = broad(grad[k : k + 1, :])
            s = times(g if carried is None else g - carried, d_ref[k])
            solved[k : k + 1, :] = s[0:1]
            if k < count - 1:
                carried = times(s, c_ref[k])

    def zero_back():
        later = None
        for k in reversed(range(count)):
            r = broad(solved[k : k + 1, :])
            if later is not None:
                r = r - times_t(later, c_ref[k])
            later = times_t(r, d_ref[k])
            update[k : k + 1, :] = later[0:1]

    def pick_odd(if_odd, if_even):
        return jnp.where(odd == 1, if_odd, if_even)

    def inner_step(it, carry):
        first = it == 0
        damp = jnp.where(first, low_damp, high_damp)
        cameras = every[it].reshape(n_c * count, width)
        eliminate_points(
            True, cameras, pick, pick_t, cj_ref, pj_ref, res_ref,
            jnp.concatenate([damp] * 2, axis=1), dense, seen, parts,
        )

        for i in reversed(range(1, n_c)):
            to = apart(i)
            remote(
                dense.at[pl.ds(pl.multiple_of(to * count, count), count)], landed.at[it, i],
                rs_send.at[it], rs_recv.at[it], to, me_p,
            ).start()
        landed[it, 0] = dense[pl.ds(pl.multiple_of(me_c * count, count), count), :]

        @pl.when(first)
        def _():
            lax.fori_loop(1, count // steps, map_back, 0)
            e_ref[odd, mine_rows] = runs[0:half]
            core_copy(e_ref, odd, 2).start()
            pair_copy(t_ref, 0).wait()
            core_copy(t_ref, 1 - odd, 1).start()

        settle(landed.at[it, pl.ds(1, n_c - 1)], rs_send.at[it], rs_recv.at[it])

        wide = jnp.concatenate([damp] * (width // damp.shape[1]), axis=1)
        mine = jnp.sum(landed[it], axis=0) + jnp.where(me_p == 0, 1.0, 0.0) * (wide * own[it])

        @pl.when(first)
        def _():
            settle(m_ref.at[:, :, mine_rows], m_send, m_recv)

        def reach(which):
            acc = None
            for k in range(count):
                new = spread(mine[k : k + 1, :], m_ref.at[k, which])
                acc = new if acc is None else acc + new
            return lane_sum(acc)

        told[it, me_p, 0:1] = -reach(1)
        told[it, me_p, 1:2] = reach(0)
        piece[it, me_p] = mine
        pair_rows = pl.ds(0, 2)
        words = told.at[it, me_p, pair_rows]
        for i in reversed(range(n_p)):
            to = lax.rem(me_p + i, n_p)
            remote(words, near.at[it, me_p, pair_rows], near_send.at[it], near_recv.at[it], beside, to).start()
            if i:
                remote(words, words, told_send.at[it], told_recv.at[it], me_c, to).start()
        for i in range(1, n_p):
            remote(
                piece.at[it, me_p], piece.at[it, me_p], pts_send.at[it], pts_recv.at[it], me_c, lax.rem(me_p + i, n_p)
            ).start()

        @pl.when(first)
        def _():
            pair_copy(e_ref, 1).start()
            core_copy(t_ref, odd, 0).wait()
            core_copy(t_ref, 1 - odd, 1).wait()

            @pl.when(inner_group)
            def _():
                ahead = t_ref[0, mine_rows]
                high, low = halves(t_ref[1])
                p_ref[own_slot, mine_rows] = stacked(dot_rows, ahead, high) + stacked(dot_rows, ahead, low)
                pass_copy(own_slot).start()
                far_each(lambda to: to <= group + 1, lambda copy: copy.start())

        settle(near.at[it, :, pair_rows], near_send.at[it], near_recv.at[it])
        settle(told.at[it, pl.ds(0, n_p - 1), pair_rows], told_send.at[it], told_recv.at[it])
        heard = jnp.sum(told[it, :, 0:2], axis=0)
        other = jnp.sum(near[it, :, 0:2], axis=0)
        f_own, b_own = heard[0:1], heard[1:2]
        f_other, b_other = other[0:1], other[1:2]
        f_a, f_b = pick_odd(f_other, f_own), pick_odd(f_own, f_other)
        b_a, b_b = pick_odd(b_other, b_own), pick_odd(b_own, b_other)

        top = pl.ds(0, 1)

        def group_share(ref, send, recv):
            for i in reversed(range(1, n_g)):
                part = ref.at[group, top]
                remote(part, part, send, recv, 2 * lax.rem(group + i, n_g) + odd, me_p).start()

        def group_await(ref, send, recv):
            settle(ref.at[pl.ds(0, n_g - 1), top], send, recv)

        group_f[group, 0:1] = row_times(f_a, t_ref.at[1]) + f_b

        def ring_copy():
            return remote(
                ring_out.at[top], ring_in.at[top], ring_send, ring_recv, 2 * lax.rem(group + 1, n_g) + odd, me_p
            )

        def fetch_e():
            pair_copy(e_ref, 1).wait()
            core_copy(e_ref, 1 - odd, 3).start()

        @pl.when(first)
        def _():
            @pl.when(group == 0)
            def _():
                ring_out[0:1] = group_f[group, 0:1]
                ring_copy().start()

        @pl.when(jnp.logical_not(first))
        def _():
            group_share(group_f, f_send, f_recv)

        settle(piece.at[it, pl.ds(0, n_p - 1)], pts_send.at[it], pts_recv.at[it])
        zero_ahead(jnp.sum(piece[it], axis=0))

        @pl.when(first)
        def _():
            @pl.when(group >= n_g // 2)
            def _():
                fetch_e()

            @pl.when(group == 0)
            def _():
                link[0:1] = jnp.zeros((1, width), F32)

            @pl.when(group > 0)
            def _():
                ring_copy().wait_recv()
                link[0:1] = ring_in[0:1]

            @pl.when(inner_group)
            def _():
                pass_copy(own_slot).wait()
                ring_out[0:1] = group_f[group, 0:1] + row_times(link[0:1, :], p_ref.at[own_slot])
                ring_copy().start()
                far_each(lambda to: to > group + 1, lambda copy: copy.start())

            @pl.when(group < n_g // 2)
            def _():
                fetch_e()

            core_copy(e_ref, odd, 2).wait()
            core_copy(e_ref, 1 - odd, 3).wait()

        @pl.when(jnp.logical_not(first))
        def _():
            group_await(group_f, f_send, f_recv)
            link[0:1] = jnp.where(group == 0, 0.0, group_f[0, 0:1])
            for j in range(1, n_g - 1):
                @pl.when(group > j)
                def _():
                    link[0:1] = group_f[j, 0:1] + row_times(link[0:1, :], p_ref.at[j - 1])

        entered = link[0:1, :]
        column = to_column(entered)
        t_b = column_times(column, t_ref.at[0]) + f_a
        back_b = b_b - row_times(t_b, e_ref.at[1])
        back_a = b_a - column_times(column, e_ref.at[0])
        backs = group_b.at[it]
        backs[group, 0:1] = back_a + row_times_t(back_b, t_ref.at[0])
        group_share(backs, b_send.at[it], b_recv.at[it])

        zero_back()
        column = to_column(pick_odd(t_b, entered))
        fixed = update[...] - jnp.concatenate([column_times(column, m_ref.at[k, 0]) for k in range(count)], axis=0)

        @pl.when(first)
        def _():
            far_arrive(lambda source: group < source)
            pass_arrive(lambda source: group < source)

        group_await(backs, b_send.at[it], b_recv.at[it])

        link[0:1] = jnp.where(group == n_g - 1, 0.0, backs[n_g - 1, 0:1])
        for j in reversed(range(1, n_g - 1)):
            @pl.when(group < j)
            def _():
                link[0:1] = backs[j, 0:1] + row_times_t(link[0:1, :], p_ref.at[j - 1])

        entered = link[0:1, :]
        later = pick_odd(entered, back_b + row_times_t(entered, t_ref.at[1]))
        column = to_column(later)
        fixed = fixed + jnp.concatenate([column_times(column, m_ref.at[k, 1]) for k in range(count)], axis=0)
        own[it + 1] = own[it] - fixed
        share_camera(it + 1)

        @pl.when(first)
        def _():
            @pl.when(group < n_g - 1)
            def _():
                ring_copy().wait_send()

            far_arrive(lambda source: group > source)
            pass_arrive(lambda source: group > source)

            @pl.when(inner_group)
            def _():
                far_each(lambda to: to >= 0, lambda copy: copy.wait_send())

        await_cameras(it + 1)
        return carry

    lax.fori_loop(0, ITERS, inner_step, 0)
    cam_out[...] = own[ITERS]
    cameras = every[ITERS].reshape(n_c * count, width)
    eliminate_points(
        False, cameras, pick, pick_t, cj_ref, pj_ref, res_ref,
        jnp.concatenate([high_damp] * 2, axis=1), point_out, seen, parts,
    )


def paired_shards(n_c, n_p, cam_jac, point_jac, residual, obs_cam, damp_exp, cam_step, diag_inverse, coupling):
    blocks, observers = obs_cam.shape
    count, width = cam_step.shape
    total_blocks = count * n_c
    pairs = observers // 2
    rows = pairs * blocks
    n_g = n_c // 2
    cj, pj, obs = cam_jac.transpose(1, 0, 2), point_jac.transpose(1, 0, 2), obs_cam.T
    res = residual.reshape(blocks, 2, pairs, 128).transpose(0, 2, 1, 3).reshape(2 * rows, 128)
    sem = pltpu.SemaphoreType.DMA

    def vmem(*shape, dtype=F32):
        return pltpu.VMEM(shape, dtype)

    camera, out = pl.pallas_call(
        functools.partial(paired_kernel, n_c, n_p),
        in_specs=[ANY] * 8,
        out_specs=[VMEM, VMEM],
        out_shape=[
            jax.ShapeDtypeStruct((count, width), F32),
            jax.ShapeDtypeStruct((3, blocks, 64), F32),
        ],
        scratch_shapes=[pltpu.VMEM(x.shape, x.dtype) for x in (obs, damp_exp, cj, pj, res, diag_inverse, coupling)]
        + [
            vmem(count, width // 2, width),
            vmem(count, 2, width, width),
            vmem(2, width, width),
            vmem(2, width, width),
            vmem(n_g - 2, width, width),
            vmem(width // 2, width),
            vmem(width, width),
            vmem(2 * rows, 3 * total_blocks, dtype=BF16),
            vmem(total_blocks, 2 * rows, dtype=BF16),
            vmem(2 * rows, width),
            vmem(2, 2 * rows, width, dtype=BF16),
            vmem(total_blocks, width),
            vmem(ITERS + 1, count, width),
            vmem(ITERS + 1, n_c, count, width),
            vmem(ITERS, n_c, count, width),
            vmem(ITERS, n_p, count, width),
            vmem(ITERS, n_p, 8, width),
            vmem(ITERS, n_p, 8, width),
            vmem(count, width),
            vmem(count, width),
            vmem(n_g, 8, width),
            vmem(ITERS, n_g, 8, width),
            vmem(8, width),
            vmem(8, width),
            vmem(8, width),
            sem((6,)), sem((2, count // 2)), sem((ITERS + 1,)), sem((ITERS + 1,)),
            sem((ITERS,)), sem((ITERS,)), sem((ITERS,)), sem((ITERS,)), sem((ITERS,)), sem((ITERS,)),
            sem((ITERS,)), sem((ITERS,)), sem(()), sem(()), sem((ITERS,)), sem((ITERS,)), sem(()), sem(()),
            sem((2,)), sem((2,)), sem((4,)), sem((4,)),
            sem((n_g,)), sem((n_g - 2,)), sem((n_g - 2,)), sem((n_g - 2,)), sem(()), sem(()),
        ],
        compiler_params=pltpu.CompilerParams(
            collective_id=0, has_side_effects=True, vmem_limit_bytes=60 << 20
        ),
        name="camera_steps",
    )(obs, damp_exp, cam_step, cj, pj, res, diag_inverse, coupling)
    return camera, out.transpose(1, 0, 2)


def solution(mesh):
    in_specs = (
        P(("chain", "pts"), None, None),
        P(("chain", "pts"), None, None),
        P(("chain", "pts"), None, None),
        P(("chain", "pts"), None),
        P(),
        P("chain", None),
        P("chain", None, None),
        P("chain", None, None),
    )
    out_specs = (P("chain", None), P(("chain", "pts"), None, None))
    n_c, n_p = mesh.shape["chain"], mesh.shape["pts"]
    paired = n_c in (8, 16) and n_p % 2 == 0
    inner = functools.partial(paired_shards if paired else shards, n_c, n_p)
    return jax.shard_map(inner, mesh=mesh, in_specs=in_specs, out_specs=out_specs, check_vma=False)
```

```python
import functools

import jax
import jax.numpy as jnp
from jax import lax
from jax.experimental import pallas as pl
from jax.experimental.pallas import tpu as pltpu
from jax.sharding import PartitionSpec as P

ITERS = 2
MESH = pl.DeviceIdType.MESH
F32, BF16 = jnp.float32, jnp.bfloat16
VMEM = pl.BlockSpec(memory_space=pltpu.VMEM)
ANY = pl.BlockSpec(memory_space=pl.ANY)


def dot_rows(x, panel):
    return lax.dot_general(x, panel, (((1,), (0,)), ((), ())), preferred_element_type=F32)


def dot_cols(x, panel):
    return lax.dot_general(x, panel, (((1,), (1,)), ((), ())), preferred_element_type=F32)


def halves(x):
    high = x.astype(BF16)
    return high, (x - high.astype(F32)).astype(BF16)


def thirds(x):
    high = x.astype(BF16)
    rest = x - high.astype(F32)
    mid = rest.astype(BF16)
    return high, mid, (rest - mid.astype(F32)).astype(BF16)


def eliminate(adjoint_out, cameras, pick_ref, pick_t_ref, cj_ref, pj_ref, res_ref, damp, out_ref, seen, parts):
    rows = res_ref.shape[1]
    blocks = rows // 4
    high, mid, low = thirds(cameras)
    pick = pick_ref[...]
    seen[...] = (dot_rows(pick, low) + dot_rows(pick, mid)) + dot_rows(pick, high)
    step = 16
    left = lax.broadcasted_iota(jnp.int32, (step, 128), 1) < 64

    def swap(x):
        return pltpu.roll(x, 64, 1)

    def chunk(i, carry):
        at = pl.multiple_of(i * step, step)
        misfits, points = [], []
        hess = [None] * 6
        target = [None] * 3
        pairs = ((0, 0), (0, 1), (0, 2), (1, 1), (1, 2), (2, 2))
        for tp in range(4):
            here = pl.ds(tp * blocks + at, step)
            there = pl.ds(rows + tp * blocks + at, step)
            cams = []
            for c in range(3):
                even = seen[here, c * 128 : (c + 1) * 128]
                odd = seen[there, c * 128 : (c + 1) * 128]
                cams.append(jnp.where(left, even, swap(odd)))
                cams.append(jnp.where(left, swap(even), odd))
            for a in range(2):
                miss = res_ref[a, here, :]
                for m in range(6):
                    miss = miss + cj_ref[6 * a + m, here, :].astype(F32) * cams[m]
                terms = [pj_ref[3 * a + n, here, :].astype(F32) for n in range(3)]
                misfits.append(miss)
                points.append(terms)
                for e, (n, k) in enumerate(pairs):
                    new = terms[n] * terms[k]
                    hess[e] = new if hess[e] is None else hess[e] + new
                for n in range(3):
                    new = terms[n] * miss
                    target[n] = new if target[n] is None else target[n] + new
        hess = [h + swap(h) for h in hess]
        ta, tb, tc = [t + swap(t) for t in target]
        aa, ab, ac, bb, bc, cc = hess
        aa, bb, cc = aa + damp, bb + damp, cc + damp
        cof_aa = bb * cc - bc * bc
        cof_ab = ac * bc - ab * cc
        cof_ac = ab * bc - ac * bb
        cof_bb = aa * cc - ac * ac
        cof_bc = ab * ac - aa * bc
        cof_cc = aa * bb - ab * ab
        det = aa * cof_aa + ab * cof_ab + ac * cof_ac
        sol = (
            (cof_aa * ta + cof_ab * tb + cof_ac * tc) / det,
            (cof_ab * ta + cof_bb * tb + cof_bc * tc) / det,
            (cof_ac * ta + cof_bc * tb + cof_cc * tc) / det,
        )
        if not adjoint_out:
            for n in range(3):
                out_ref[n, pl.ds(at, step), :] = -sol[n]
            return carry
        for tp in range(4):
            here = pl.ds(tp * blocks + at, step)
            there = pl.ds(rows + tp * blocks + at, step)
            left_over = []
            for a in range(2):
                terms = points[2 * tp + a]
                left_over.append(
                    misfits[2 * tp + a]
                    - (terms[0] * sol[0] + terms[1] * sol[1] + terms[2] * sol[2])
                )
            adj = [
                cj_ref[m, here, :].astype(F32) * left_over[0]
                + cj_ref[6 + m, here, :].astype(F32) * left_over[1]
                for m in range(6)
            ]
            for c in range(3):
                span = slice(c * 128, (c + 1) * 128)
                even = jnp.where(left, adj[2 * c], swap(adj[2 * c + 1]))
                odd = jnp.where(left, swap(adj[2 * c]), adj[2 * c + 1])
                for part, value in enumerate(thirds(even)):
                    parts[part, here, span] = value
                for part, value in enumerate(thirds(odd)):
                    parts[part, there, span] = value
        return carry

    lax.fori_loop(0, blocks // step, chunk, 0)
    if adjoint_out:
        pick_t = pick_t_ref[...]
        out_ref[...] = (
            dot_rows(pick_t, parts[2]) + dot_rows(pick_t, parts[1])
        ) + dot_rows(pick_t, parts[0])


def split_row(v):
    row = lax.broadcasted_iota(jnp.int32, v.shape, 0)
    high = v.astype(BF16).astype(F32)
    rest = v - high
    mid = rest.astype(BF16).astype(F32)
    low = rest - mid
    return jnp.where(row == 0, high, jnp.where(row == 1, mid, jnp.where(row == 2, low, 0.0))).astype(BF16)


def total(y):
    return jnp.broadcast_to(jnp.sum(y, axis=0, keepdims=True), y.shape)


def times(v, panel):
    return total(dot_rows(split_row(v), panel))


def times_t(v, panel):
    return total(dot_cols(split_row(v), panel))


def stacked(dot, x, panel):
    rows = x.shape[0]
    both = dot(jnp.concatenate(halves(x), axis=0), panel)
    return both[:rows] + both[rows:]


def whole_kernel(
    n_c, n_p,
    order_ref, cam_ref, damp_ref, cj_hbm, pj_hbm, res_hbm, d_hbm, c_hbm,
    cam_out, point_out,
    cj_ref, pj_ref, res_ref, d_ref, c_ref, wh_ref, wl_ref, xh_ref, xl_ref, rh_ref, rl_ref, run_f, run_b,
    pick, pick_t, seen, parts, dense, own, every,
    landed, piece, grad, solved, update, carry_in, carry_out, first_in, first_out, entry,
    run_nb, nh_ref, nl_ref, ph_ref, pk_ref,
    load_sem, rs_send, rs_recv, pts_send, pts_recv, ring_send, ring_recv, first_send, first_recv, all_send, all_recv, nb_send, nb_recv,
):
    me_c, me_p = lax.axis_index("chain"), lax.axis_index("pts")
    count, width = cam_ref.shape
    rows = res_ref.shape[1]
    loads = [
        pltpu.make_async_copy(src, dst, load_sem.at[i])
        for i, (src, dst) in enumerate(
            ((d_hbm, d_ref), (c_hbm, c_ref), (cj_hbm, cj_ref), (pj_hbm, pj_ref), (res_hbm, res_ref))
        )
    ]
    for load in loads:
        load.start()

    barrier = pltpu.get_barrier_semaphore()

    @pl.loop(1, n_c)
    def _(i):
        pl.semaphore_signal(
            barrier, inc=1, device_id=(lax.rem(me_c + i, n_c), me_p), device_id_type=MESH
        )

    for i in range(1, n_p):
        pl.semaphore_signal(
            barrier, inc=1, device_id=(me_c, lax.rem(me_p + i, n_p)), device_id_type=MESH
        )
    pl.semaphore_wait(barrier, n_c + n_p - 2)

    def all_copy(turn, i):
        return pltpu.make_async_remote_copy(
            src_ref=own.at[turn],
            dst_ref=every.at[turn, me_c],
            send_sem=all_send.at[turn, i],
            recv_sem=all_recv.at[turn, i],
            device_id=(lax.rem(me_c + i, n_c), me_p),
            device_id_type=MESH,
        )

    def share_camera(turn):
        @pl.loop(1, n_c)
        def _(i):
            all_copy(turn, i).start()

        every[turn, me_c] = own[turn]

    def await_cameras(turn):
        @pl.loop(1, n_c)
        def _(i):
            all_copy(turn, i).wait()

    own[0] = cam_ref[...]
    share_camera(0)

    cams = lax.broadcasted_iota(jnp.int32, pick_t.shape, 0)
    chosen = jnp.where(cams == jnp.broadcast_to(order_ref[...], pick_t.shape), 1.0, 0.0)
    pick_t[...] = chosen.astype(BF16)
    pick[...] = chosen.T.astype(BF16)

    unit = (
        lax.broadcasted_iota(jnp.int32, (width, width), 0)
        == lax.broadcasted_iota(jnp.int32, (width, width), 1)
    ).astype(F32)
    run_f[...] = unit
    run_b[...] = unit

    def map_ahead(k, carry):
        made = -stacked(dot_rows, run_f[...], d_ref[k])
        high, low = halves(made)
        wh_ref[k] = high
        wl_ref[k] = low
        run_f[...] = stacked(dot_rows, made, c_ref[k])
        return carry

    def map_back(i, carry):
        k = count - 1 - i
        made = stacked(dot_cols, -stacked(dot_cols, run_b[...], c_ref[k]), d_ref[k])
        run_b[...] = made
        high, low = halves(made)
        xh_ref[k] = high
        xl_ref[k] = low
        return carry

    odd = lax.rem(me_c, 2)
    swap_maps = pltpu.make_async_remote_copy(
        src_ref=run_f, dst_ref=run_nb, send_sem=nb_send, recv_sem=nb_recv,
        device_id=(me_c + 1 - 2 * odd, me_p), device_id_type=MESH,
    )

    def pair_map():
        high, low = halves(run_f[...])
        rh_ref[...] = high
        rl_ref[...] = low
        swap_maps.wait()
        mine, other = run_f[...], run_nb[...]
        nh_ref[...], nl_ref[...] = halves(other)
        early = jnp.where(odd == 1, other, mine)
        late_high, late_low = halves(jnp.where(odd == 1, mine, other))
        high, low = halves(stacked(dot_rows, early, late_high) + stacked(dot_rows, early, late_low))
        ph_ref[...] = high
        pk_ref[...] = low

    loads[0].wait()
    loads[1].wait()
    lax.fori_loop(0, count, map_ahead, 0)
    swap_maps.start()
    for load in loads[2:]:
        load.wait()
    await_cameras(0)

    def zero_ahead():
        carried = None
        for k in range(count):
            g = jnp.broadcast_to(grad[k : k + 1, :], carry_in.shape[2:])
            s = times(g if carried is None else g - carried, d_ref[k])
            solved[k : k + 1, :] = s[0:1]
            if k < count - 1:
                carried = times(s, c_ref[k])

    def zero_back():
        later = None
        for k in reversed(range(count)):
            r = jnp.broadcast_to(solved[k : k + 1, :], carry_in.shape[2:])
            if later is not None:
                r = r - times_t(later, c_ref[k])
            later = times_t(r, d_ref[k])
            update[k : k + 1, :] = later[0:1]

    def reach(vectors, high_ref, low_ref):
        acc = None
        for k in range(count):
            x = split_row(jnp.broadcast_to(vectors[k : k + 1, :], carry_in.shape[2:]))
            new = dot_cols(x, high_ref[k]) + dot_cols(x, low_ref[k])
            acc = new if acc is None else acc + new
        return -total(acc)

    def correct(x, out, high_ref, low_ref):
        for k in range(count):
            y = dot_rows(x, high_ref[k]) + dot_rows(x, low_ref[k])
            out[k : k + 1, :] = out[k : k + 1, :] + jnp.sum(y, axis=0, keepdims=True)

    def inner_step(it, carry):
        damp = damp_ref[it]
        cameras = every[it].reshape(n_c * count, width)
        eliminate(True, cameras, pick, pick_t, cj_ref, pj_ref, res_ref, damp[:, :128], dense, seen, parts)

        def rs_copy(i):
            to = lax.rem(me_c + i, n_c)
            return pltpu.make_async_remote_copy(
                src_ref=dense.at[pl.ds(pl.multiple_of(to * count, count), count)],
                dst_ref=landed.at[it, i],
                send_sem=rs_send.at[it, i],
                recv_sem=rs_recv.at[it, i],
                device_id=(to, me_p),
                device_id_type=MESH,
            )

        @pl.loop(1, n_c)
        def _(i):
            rs_copy(i).start()

        landed[it, 0] = dense[pl.ds(pl.multiple_of(me_c * count, count), count), :]

        @pl.when(it == 0)
        def _():
            lax.fori_loop(0, count, map_back, 0)

        @pl.loop(1, n_c)
        def _(i):
            rs_copy(i).wait()

        mine = jnp.sum(landed[it], axis=0)

        def pts_copy(i):
            return pltpu.make_async_remote_copy(
                src_ref=piece.at[it, me_p],
                dst_ref=piece.at[it, me_p],
                send_sem=pts_send.at[it, i],
                recv_sem=pts_recv.at[it, i],
                device_id=(me_c, lax.rem(me_p + i, n_p)),
                device_id_type=MESH,
            )

        piece[it, me_p] = mine
        for i in range(1, n_p):
            pts_copy(i).start()

        @pl.when(it == 0)
        def _():
            pair_map()

        for i in range(1, n_p):
            pts_copy(i).wait()
        grad[...] = jnp.sum(piece[it], axis=0) + damp * own[it]

        def hand(way):
            return pltpu.make_async_remote_copy(
                src_ref=first_out.at[it, way], dst_ref=first_in.at[it, way],
                send_sem=first_send.at[it, way], recv_sem=first_recv.at[it, way],
                device_id=(me_c + 1 - 2 * odd, me_p), device_id_type=MESH,
            )

        def ring(way, far):
            to = lax.rem(me_c + (n_c - far if way else far), n_c)
            return pltpu.make_async_remote_copy(
                src_ref=carry_out.at[it, way], dst_ref=carry_in.at[it, way],
                send_sem=ring_send.at[it, way, far - 1], recv_sem=ring_recv.at[it, way],
                device_id=(to, me_p), device_id_type=MESH,
            )

        def seat(way):
            turn = n_c - 1 - me_c if way else me_c
            return lax.rem(turn, 2) == 1, turn // 2

        def pass_on(way, reached, map_high, map_low, sweep):
            second, group = seat(way)
            dot = dot_cols if way else dot_rows

            def arrive():
                @pl.when(group == 0)
                def _():
                    carry_in[it, way] = jnp.zeros(carry_in.shape[2:], F32)

                @pl.when(group > 0)
                def _():
                    ring(way, 2).wait_recv()

                return carry_in[it, way]

            first_out[it, way] = reached

            @pl.when(jnp.logical_not(second))
            def _():
                hand(way).start()
                sweep()
                entry[...] = arrive()

            @pl.when(second)
            def _():
                @pl.when(group >= 2)
                def _():
                    sweep()

                hand(way).wait_recv()
                given = first_in[it, way]
                x = split_row(given)
                both = first_out[it, way] + total(dot_rows(x, map_high[...]) + dot_rows(x, map_low[...]))
                x = split_row(arrive())
                carry_out[it, way] = both + total(dot(x, ph_ref[...]) + dot(x, pk_ref[...]))

                @pl.when(group < n_c // 2 - 1)
                def _():
                    ring(way, 2).start()
                    ring(way, 1).start()

                entry[...] = given + total(dot(x, nh_ref[...]) + dot(x, nl_ref[...]))

                @pl.when(group < 2)
                def _():
                    sweep()

            return split_row(entry[...])

        def drain(way):
            second, group = seat(way)

            @pl.when(jnp.logical_not(second))
            def _():
                hand(way).wait_send()

            @pl.when(jnp.logical_and(second, group < n_c // 2 - 1))
            def _():
                ring(way, 2).wait_send()
                ring(way, 1).wait_send()

        x = pass_on(0, reach(grad, xh_ref, xl_ref), rh_ref, rl_ref, zero_ahead)
        correct(x, solved, wh_ref, wl_ref)
        x = pass_on(1, reach(solved, wh_ref, wl_ref), xh_ref.at[0], xl_ref.at[0], zero_back)
        correct(x, update, xh_ref, xl_ref)
        own[it + 1] = own[it] - update[...]
        share_camera(it + 1)

        drain(0)
        drain(1)
        await_cameras(it + 1)
        return carry

    lax.fori_loop(0, ITERS, inner_step, 0)
    cam_out[...] = own[ITERS]
    cameras = every[ITERS].reshape(n_c * count, width)
    eliminate(
        False, cameras, pick, pick_t, cj_ref, pj_ref, res_ref, damp_ref[ITERS - 1][:, :128], point_out, seen, parts
    )


def shards(n_c, n_p, cam_jac, point_jac, residual, obs_cam, damp_exp, cam_step, diag_inverse, coupling):
    blocks, observers = obs_cam.shape
    count, width = cam_step.shape
    total_blocks = count * n_c
    pairs = observers // 2
    rows = pairs * blocks

    def by_pair(x):
        comps = x.shape[1]
        return x.reshape(blocks, comps, pairs, 128).transpose(1, 2, 0, 3).reshape(comps, rows, 128)

    cj, pj, res = by_pair(cam_jac), by_pair(point_jac), by_pair(residual)
    order = obs_cam.reshape(blocks, pairs, 2).transpose(2, 1, 0).reshape(1, -1)
    wide = jnp.tile(jnp.exp2(damp_exp.astype(F32)), (1, 6))[:, None, :]
    panel = pltpu.VMEM((count, width, width), BF16)
    square = (width, width)
    sem = pltpu.SemaphoreType.DMA
    camera, out = pl.pallas_call(
        functools.partial(whole_kernel, n_c, n_p),
        in_specs=[VMEM] * 3 + [ANY] * 5,
        out_specs=[VMEM, VMEM],
        out_shape=[
            jax.ShapeDtypeStruct((count, width), F32),
            jax.ShapeDtypeStruct((3, blocks, 128), F32),
        ],
        scratch_shapes=[pltpu.VMEM(x.shape, x.dtype) for x in (cj, pj, res)]
        + [panel] * 6
        + [pltpu.VMEM(square, BF16)] * 2
        + [pltpu.VMEM(square, F32)] * 2
        + [
            pltpu.VMEM((2 * rows, total_blocks), BF16),
            pltpu.VMEM((total_blocks, 2 * rows), BF16),
            pltpu.VMEM((2 * rows, width), F32),
            pltpu.VMEM((3, 2 * rows, width), BF16),
            pltpu.VMEM((total_blocks, width), F32),
            pltpu.VMEM((ITERS + 1, count, width), F32),
            pltpu.VMEM((ITERS + 1, n_c, count, width), F32),
            pltpu.VMEM((ITERS, n_c, count, width), F32),
            pltpu.VMEM((ITERS, n_p, count, width), F32),
            pltpu.VMEM((count, width), F32),
            pltpu.VMEM((count, width), F32),
            pltpu.VMEM((count, width), F32),
            pltpu.VMEM((ITERS, 2, 8, width), F32),
            pltpu.VMEM((ITERS, 2, 8, width), F32),
            pltpu.VMEM((ITERS, 2, 8, width), F32),
            pltpu.VMEM((ITERS, 2, 8, width), F32),
            pltpu.VMEM((8, width), F32),
            pltpu.VMEM(square, F32),
            pltpu.VMEM(square, BF16),
            pltpu.VMEM(square, BF16),
            pltpu.VMEM(square, BF16),
            pltpu.VMEM(square, BF16),
            sem((5,)), sem((ITERS, n_c)), sem((ITERS, n_c)), sem((ITERS, n_p)), sem((ITERS, n_p)),
            sem((ITERS, 2, 2)), sem((ITERS, 2)), sem((ITERS, 2)), sem((ITERS, 2)),
            sem((ITERS + 1, n_c)), sem((ITERS + 1, n_c)), sem(()), sem(()),
        ],
        compiler_params=pltpu.CompilerParams(
            collective_id=0, has_side_effects=True, vmem_limit_bytes=48 << 20
        ),
        name="camera_steps",
    )(order, cam_step, wide, cj, pj, res, diag_inverse, coupling)
    return camera, out[:, :, :64].transpose(1, 0, 2)


def lanes(x, c):
    return x[:, c * 128 : (c + 1) * 128]


def to_column(x):
    return jnp.concatenate(
        [jnp.broadcast_to(lanes(x, c), (128, 128)).T for c in range(x.shape[1] // 128)], axis=0
    )


def column_times(column, m):
    return jnp.concatenate(
        [jnp.sum(m[:, c * 128 : (c + 1) * 128] * column, axis=0, keepdims=True) for c in range(m.shape[1] // 128)],
        axis=1,
    )


def spread(x, m):
    acc = None
    for c in range(m.shape[1] // 128):
        new = m[:, c * 128 : (c + 1) * 128] * lanes(x, c)
        acc = new if acc is None else acc + new
    return acc


def lane_sum(acc):
    parts = jnp.concatenate(thirds(acc), axis=1)
    return dot_cols(jnp.ones((8, parts.shape[1]), BF16), parts)[0:1]


def row_times(x, m):
    return column_times(to_column(x), m)


def row_times_t(x, m):
    return lane_sum(spread(x, m))


def eliminate_points(adjoint_out, cameras, pick_ref, pick_t_ref, cj_ref, pj_ref, res_ref, damp, out_ref, seen, parts):
    blocks = cj_ref.shape[1]
    pairs = cj_ref.shape[2] // 128
    rows = pairs * blocks
    seen[...] = dot_rows(pick_ref[...], jnp.concatenate(thirds(cameras), axis=0))
    step = 16
    left = lax.broadcasted_iota(jnp.int32, (step, 128), 1) < 64

    def swap(x):
        return pltpu.roll(x, 64, 1)

    def chunk(i, carry):
        at = pl.multiple_of(i * step, step)
        body = pl.ds(at, step)
        misfits, points = [], []
        hess = [None] * 6
        target = [None] * 3
        order = ((0, 0), (0, 1), (0, 2), (1, 1), (1, 2), (2, 2))
        for tp in range(pairs):
            here = pl.ds(tp * blocks + at, step)
            there = pl.ds(rows + tp * blocks + at, step)
            span = slice(tp * 128, (tp + 1) * 128)
            cams = []
            for c in range(3):
                even = seen[here, c * 128 : (c + 1) * 128]
                odd = seen[there, c * 128 : (c + 1) * 128]
                cams.append(jnp.where(left, even, swap(odd)))
                cams.append(jnp.where(left, swap(even), odd))
            for a in range(2):
                miss = res_ref[pl.ds(at * 2 * pairs + tp * 2 + a, step, stride=2 * pairs), :]
                for m in range(6):
                    miss = miss + cj_ref[6 * a + m, body, span].astype(F32) * cams[m]
                terms = [pj_ref[3 * a + n, body, span].astype(F32) for n in range(3)]
                misfits.append(miss)
                points.append(terms)
                for e, (n, k) in enumerate(order):
                    new = terms[n] * terms[k]
                    hess[e] = new if hess[e] is None else hess[e] + new
                for n in range(3):
                    new = terms[n] * miss
                    target[n] = new if target[n] is None else target[n] + new
        hess = [h + swap(h) for h in hess]
        ta, tb, tc = [t + swap(t) for t in target]
        aa, ab, ac, bb, bc, cc = hess
        aa, bb, cc = aa + damp, bb + damp, cc + damp
        cof_aa = bb * cc - bc * bc
        cof_ab = ac * bc - ab * cc
        cof_ac = ab * bc - ac * bb
        cof_bb = aa * cc - ac * ac
        cof_bc = ab * ac - aa * bc
        cof_cc = aa * bb - ab * ab
        det = aa * cof_aa + ab * cof_ab + ac * cof_ac
        sol = (
            (cof_aa * ta + cof_ab * tb + cof_ac * tc) / det,
            (cof_ab * ta + cof_bb * tb + cof_bc * tc) / det,
            (cof_ac * ta + cof_bc * tb + cof_cc * tc) / det,
        )
        if not adjoint_out:
            for n in range(3):
                out_ref[n, body, :] = -sol[n][:, : out_ref.shape[2]]
            return carry
        for tp in range(pairs):
            here = pl.ds(tp * blocks + at, step)
            there = pl.ds(rows + tp * blocks + at, step)
            span = slice(tp * 128, (tp + 1) * 128)
            left_over = []
            for a in range(2):
                terms = points[2 * tp + a]
                left_over.append(
                    misfits[2 * tp + a]
                    - (terms[0] * sol[0] + terms[1] * sol[1] + terms[2] * sol[2])
                )
            adj = [
                cj_ref[m, body, span].astype(F32) * left_over[0]
                + cj_ref[6 + m, body, span].astype(F32) * left_over[1]
                for m in range(6)
            ]
            for c in range(3):
                out = slice(c * 128, (c + 1) * 128)
                even = jnp.where(left, adj[2 * c], swap(adj[2 * c + 1]))
                odd = jnp.where(left, swap(adj[2 * c]), adj[2 * c + 1])
                for part, value in enumerate(halves(even)):
                    parts[part, here, out] = value
                for part, value in enumerate(halves(odd)):
                    parts[part, there, out] = value
        return carry

    lax.fori_loop(0, blocks // step, chunk, 0)
    if adjoint_out:
        pick_t = pick_t_ref[...]
        out_ref[...] = dot_rows(pick_t, parts[1]) + dot_rows(pick_t, parts[0])


def paired_kernel(
    n_c, n_p,
    obs_hbm, exp_hbm, cam_hbm, cj_hbm, pj_hbm, res_hbm, d_hbm, c_hbm,
    cam_out, point_out,
    obs_ref, exp_ref, cj_ref, pj_ref, res_ref, d_ref, c_ref,
    w_ref, m_ref, t_ref, e_ref, p_ref, run, runs,
    pick, pick_t, seen, parts, dense, own, every, landed, piece, told, near,
    solved, update, group_f, group_b, ring_out, ring_in, link,
    load_sem, panel_sem, all_send, all_recv, rs_send, rs_recv, pts_send, pts_recv, told_send, told_recv,
    near_send, near_recv, f_send, f_recv, b_send, b_recv, m_send, m_recv,
    pair_send, pair_recv, core_send, core_recv, far_send, far_recv, pass_send, pass_recv, ring_send, ring_recv,
):
    me_c, me_p = lax.axis_index("chain"), lax.axis_index("pts")
    n_g = n_c // 2
    group, odd = me_c // 2, lax.rem(me_c, 2)
    beside = me_c + 1 - 2 * odd
    twin = me_p + 1 - 2 * lax.rem(me_p, 2)
    count, width = cam_hbm.shape
    half = width // 2
    steps = 2

    def apart(i):
        to, bit = 0, 1
        while bit < n_c:
            mine = lax.rem(me_c // bit, 2)
            to = to + bit * (1 - mine if i & bit else mine)
            bit = 2 * bit
        return to

    def settle(ref, *sems):
        for sem in sems:
            pltpu.make_async_copy(ref, ref, sem).wait()
    mine_rows = pl.ds(pl.multiple_of(lax.rem(me_p, 2) * half, 8), half)

    barrier = pltpu.get_barrier_semaphore()

    for i in range(1, n_c):
        pl.semaphore_signal(
            barrier, inc=1, device_id=(lax.rem(me_c + i, n_c), me_p), device_id_type=MESH
        )
    for i in range(1, n_p):
        to = lax.rem(me_p + i, n_p)
        pl.semaphore_signal(barrier, inc=1, device_id=(me_c, to), device_id_type=MESH)
        pl.semaphore_signal(barrier, inc=1, device_id=(beside, to), device_id_type=MESH)

    loads = [
        pltpu.make_async_copy(src, dst, load_sem.at[i])
        for i, (src, dst) in enumerate(
            (
                (cam_hbm, own.at[0]), (obs_hbm, obs_ref), (exp_hbm, exp_ref),
                (cj_hbm, cj_ref), (pj_hbm, pj_ref), (res_hbm, res_ref),
            )
        )
    ]

    def panel_load(k):
        at = pl.ds(k * steps, steps)
        return (
            pltpu.make_async_copy(d_hbm.at[at], d_ref.at[at], panel_sem.at[0, k]),
            pltpu.make_async_copy(c_hbm.at[at], c_ref.at[at], panel_sem.at[1, k]),
        )

    for k in range(count // steps):
        for load in panel_load(k):
            load.start()
        if k == 0:
            for load in loads[:3]:
                load.start()
    for load in loads[3:]:
        load.start()

    def remote(src, dst, send, recv, chain, pts):
        return pltpu.make_async_remote_copy(
            src_ref=src, dst_ref=dst, send_sem=send, recv_sem=recv,
            device_id=(chain, pts), device_id_type=MESH,
        )

    def share_camera(turn):
        for i in reversed(range(1, n_c)):
            remote(
                own.at[turn], every.at[turn, me_c], all_send.at[turn], all_recv.at[turn], apart(i), me_p
            ).start()
        every[turn, me_c] = own[turn]

    def await_cameras(turn):
        settle(every.at[turn, pl.ds(0, n_c - 1)], all_send.at[turn], all_recv.at[turn])

    def map_copy(k):
        part = m_ref.at[k, :, mine_rows]
        return remote(part, part, m_send, m_recv, me_c, twin)

    def pair_copy(ref, i):
        return remote(ref.at[odd, mine_rows], ref.at[odd, mine_rows], pair_send.at[i], pair_recv.at[i], beside, me_p)

    def core_copy(ref, seat, i):
        return remote(ref.at[seat, mine_rows], ref.at[seat, mine_rows], core_send.at[i], core_recv.at[i], me_c, twin)

    own_slot = jnp.clip(group - 1, 0, n_g - 3)

    def far_each(where, act):
        for i in range(1, n_g):
            to = lax.rem(group + i, n_g)

            @pl.when(where(to))
            def _():
                act(
                    remote(
                        p_ref.at[own_slot, mine_rows], p_ref.at[own_slot, mine_rows],
                        far_send.at[i], far_recv.at[own_slot], 2 * to + odd, me_p,
                    )
                )

    def far_arrive(where):
        for slot in range(n_g - 2):
            @pl.when(where(slot + 1))
            def _():
                remote(
                    p_ref.at[slot, mine_rows], p_ref.at[slot, mine_rows], far_send.at[0], far_recv.at[slot],
                    beside, me_p,
                ).wait_recv()
                pass_copy(slot).start()

    def pass_arrive(where):
        for slot in range(n_g - 2):
            @pl.when(where(slot + 1))
            def _():
                pass_copy(slot).wait()

    def pass_copy(slot):
        return remote(
            p_ref.at[slot, mine_rows], p_ref.at[slot, mine_rows], pass_send.at[slot], pass_recv.at[slot], me_c, twin
        )

    unit_rows = (
        lax.broadcasted_iota(jnp.int32, (half, width), 0) + lax.rem(me_p, 2) * half
        == lax.broadcasted_iota(jnp.int32, (half, width), 1)
    ).astype(F32)
    run[...] = unit_rows

    runs[0:half] = jnp.zeros((half, width), F32)
    runs[half:] = unit_rows

    def map_ahead(i, carry):
        for load in panel_load(i):
            load.wait()
        held = run[...]
        for u in range(steps):
            k = i * steps + u
            made = -stacked(dot_rows, held, d_ref[k])
            w_ref[k] = made
            held = stacked(dot_rows, made, c_ref[k])
        run[...] = held
        return carry

    def map_back(i, carry):
        held = runs[...]
        for u in range(steps):
            k = count - 1 - i * steps - u
            held = stacked(dot_cols, held, c_ref[k])
            held = -jnp.concatenate([held[:half] + w_ref[k], held[half:]], axis=0)
            held = stacked(dot_cols, held, d_ref[k])
            m_ref[k, 0, mine_rows] = held[:half]
            m_ref[k, 1, mine_rows] = held[half:]
            map_copy(k).start()
        runs[...] = held
        return carry

    lax.fori_loop(0, 1, map_ahead, 0)

    for load in loads[:3]:
        load.wait()
    obs = obs_ref[...]
    observers = obs.shape[0]
    order = jnp.concatenate(
        [obs[t : t + 1, :] for h in range(2) for t in range(h, observers, 2)], axis=1
    )
    cams = lax.broadcasted_iota(jnp.int32, pick_t.shape, 0)
    chosen = jnp.where(cams == jnp.broadcast_to(order, pick_t.shape), 1.0, 0.0)
    pick_t[...] = chosen.astype(BF16)
    pick[...] = jnp.concatenate([chosen] * 3, axis=0).T.astype(BF16)
    damps = jnp.exp2(exp_ref[...].astype(F32))
    low_damp, high_damp = damps[0:1], damps[ITERS - 1 : ITERS]

    pl.semaphore_wait(barrier, n_c - 1 + 2 * (n_p - 1))

    share_camera(0)
    lax.fori_loop(1, count // steps, map_ahead, 0)
    t_ref[odd, mine_rows] = run[...]
    pair_copy(t_ref, 0).start()
    core_copy(t_ref, odd, 0).start()
    lax.fori_loop(0, 1, map_back, 0)
    for load in loads[3:]:
        load.wait()
    await_cameras(0)

    inner_group = jnp.logical_and(group >= 1, group <= n_g - 2)

    def broad(row):
        return jnp.broadcast_to(row, (8, width))

    def zero_ahead(grad):
        carried = None
        for k in range(count):
            g = broad(grad[k : k + 1, :])
            s = times(g if carried is None else g - carried, d_ref[k])
            solved[k : k + 1, :] = s[0:1]
            if k < count - 1:
                carried = times(s, c_ref[k])

    def zero_back():
        later = None
        for k in reversed(range(count)):
            r = broad(solved[k : k + 1, :])
            if later is not None:
                r = r - times_t(later, c_ref[k])
            later = times_t(r, d_ref[k])
            update[k : k + 1, :] = later[0:1]

    def pick_odd(if_odd, if_even):
        return jnp.where(odd == 1, if_odd, if_even)

    def inner_step(it, carry):
        first = it == 0
        damp = jnp.where(first, low_damp, high_damp)
        cameras = every[it].reshape(n_c * count, width)
        eliminate_points(
            True, cameras, pick, pick_t, cj_ref, pj_ref, res_ref,
            jnp.concatenate([damp] * 2, axis=1), dense, seen, parts,
        )

        for i in reversed(range(1, n_c)):
            to = apart(i)
            remote(
                dense.at[pl.ds(pl.multiple_of(to * count, count), count)], landed.at[it, i],
                rs_send.at[it], rs_recv.at[it], to, me_p,
            ).start()
        landed[it, 0] = dense[pl.ds(pl.multiple_of(me_c * count, count), count), :]

        @pl.when(first)
        def _():
            lax.fori_loop(1, count // steps - 1, map_back, 0)
            pair_copy(t_ref, 0).wait()
            core_copy(t_ref, 1 - odd, 1).start()
            lax.fori_loop(count // steps - 1, count // steps, map_back, 0)
            e_ref[odd, mine_rows] = runs[0:half]
            core_copy(e_ref, odd, 2).start()
            core_copy(t_ref, odd, 0).wait()
            core_copy(t_ref, 1 - odd, 1).wait()

            @pl.when(inner_group)
            def _():
                ahead = t_ref[0, mine_rows]
                high, low = halves(t_ref[1])
                p_ref[own_slot, mine_rows] = stacked(dot_rows, ahead, high) + stacked(dot_rows, ahead, low)
                pass_copy(own_slot).start()
                far_each(lambda to: to <= group + 1, lambda copy: copy.start())

        settle(landed.at[it, pl.ds(1, n_c - 1)], rs_send.at[it], rs_recv.at[it])

        wide = jnp.concatenate([damp] * (width // damp.shape[1]), axis=1)
        mine = jnp.sum(landed[it], axis=0) + jnp.where(me_p == 0, 1.0, 0.0) * (wide * own[it])

        @pl.when(first)
        def _():
            settle(m_ref.at[:, :, mine_rows], m_send, m_recv)

        def reach(which):
            acc = None
            for k in range(count):
                new = spread(mine[k : k + 1, :], m_ref.at[k, which])
                acc = new if acc is None else acc + new
            return lane_sum(acc)

        told[it, me_p, 0:1] = -reach(1)
        told[it, me_p, 1:2] = reach(0)
        piece[it, me_p] = mine
        pair_rows = pl.ds(0, 2)
        words = told.at[it, me_p, pair_rows]
        for i in reversed(range(n_p)):
            to = lax.rem(me_p + i, n_p)
            remote(words, near.at[it, me_p, pair_rows], near_send.at[it], near_recv.at[it], beside, to).start()
            if i:
                remote(words, words, told_send.at[it], told_recv.at[it], me_c, to).start()
        for i in range(1, n_p):
            remote(
                piece.at[it, me_p], piece.at[it, me_p], pts_send.at[it], pts_recv.at[it], me_c, lax.rem(me_p + i, n_p)
            ).start()

        @pl.when(first)
        def _():
            pair_copy(e_ref, 1).start()

        settle(near.at[it, :, pair_rows], near_send.at[it], near_recv.at[it])
        settle(told.at[it, pl.ds(0, n_p - 1), pair_rows], told_send.at[it], told_recv.at[it])
        heard = jnp.sum(told[it, :, 0:2], axis=0)
        other = jnp.sum(near[it, :, 0:2], axis=0)
        f_own, b_own = heard[0:1], heard[1:2]
        f_other, b_other = other[0:1], other[1:2]
        f_a, f_b = pick_odd(f_other, f_own), pick_odd(f_own, f_other)
        b_a, b_b = pick_odd(b_other, b_own), pick_odd(b_own, b_other)

        top = pl.ds(0, 1)

        def group_share(ref, send, recv):
            for i in reversed(range(1, n_g)):
                part = ref.at[group, top]
                remote(part, part, send, recv, 2 * lax.rem(group + i, n_g) + odd, me_p).start()

        def group_await(ref, send, recv):
            settle(ref.at[pl.ds(0, n_g - 1), top], send, recv)

        group_f[group, 0:1] = row_times(f_a, t_ref.at[1]) + f_b

        def ring_copy():
            return remote(
                ring_out.at[top], ring_in.at[top], ring_send, ring_recv, 2 * lax.rem(group + 1, n_g) + odd, me_p
            )

        def fetch_e():
            pair_copy(e_ref, 1).wait()
            core_copy(e_ref, 1 - odd, 3).start()

        @pl.when(first)
        def _():
            @pl.when(group == 0)
            def _():
                ring_out[0:1] = group_f[group, 0:1]
                ring_copy().start()

        @pl.when(jnp.logical_not(first))
        def _():
            group_share(group_f, f_send, f_recv)

        settle(piece.at[it, pl.ds(0, n_p - 1)], pts_send.at[it], pts_recv.at[it])
        zero_ahead(jnp.sum(piece[it], axis=0))

        @pl.when(first)
        def _():
            @pl.when(group >= n_g // 2)
            def _():
                fetch_e()

            @pl.when(group == 0)
            def _():
                link[0:1] = jnp.zeros((1, width), F32)

            @pl.when(group > 0)
            def _():
                ring_copy().wait_recv()
                link[0:1] = ring_in[0:1]

            @pl.when(inner_group)
            def _():
                pass_copy(own_slot).wait()
                ring_out[0:1] = group_f[group, 0:1] + row_times(link[0:1, :], p_ref.at[own_slot])
                ring_copy().start()
                far_each(lambda to: to > group + 1, lambda copy: copy.start())

            @pl.when(group < n_g // 2)
            def _():
                fetch_e()

            core_copy(e_ref, odd, 2).wait()
            core_copy(e_ref, 1 - odd, 3).wait()

        @pl.when(jnp.logical_not(first))
        def _():
            group_await(group_f, f_send, f_recv)
            link[0:1] = jnp.where(group == 0, 0.0, group_f[0, 0:1])
            for j in range(1, n_g - 1):
                @pl.when(group > j)
                def _():
                    link[0:1] = group_f[j, 0:1] + row_times(link[0:1, :], p_ref.at[j - 1])

        entered = link[0:1, :]
        column = to_column(entered)
        t_b = column_times(column, t_ref.at[0]) + f_a
        back_b = b_b - row_times(t_b, e_ref.at[1])
        back_a = b_a - column_times(column, e_ref.at[0])
        backs = group_b.at[it]
        backs[group, 0:1] = back_a + row_times_t(back_b, t_ref.at[0])
        group_share(backs, b_send.at[it], b_recv.at[it])

        zero_back()
        column = to_column(pick_odd(t_b, entered))
        fixed = update[...] - jnp.concatenate([column_times(column, m_ref.at[k, 0]) for k in range(count)], axis=0)

        @pl.when(first)
        def _():
            far_arrive(lambda source: group < source)
            pass_arrive(lambda source: group < source)

        group_await(backs, b_send.at[it], b_recv.at[it])

        link[0:1] = jnp.where(group == n_g - 1, 0.0, backs[n_g - 1, 0:1])
        for j in reversed(range(1, n_g - 1)):
            @pl.when(group < j)
            def _():
                link[0:1] = backs[j, 0:1] + row_times_t(link[0:1, :], p_ref.at[j - 1])

        entered = link[0:1, :]
        later = pick_odd(entered, back_b + row_times_t(entered, t_ref.at[1]))
        column = to_column(later)
        fixed = fixed + jnp.concatenate([column_times(column, m_ref.at[k, 1]) for k in range(count)], axis=0)
        own[it + 1] = own[it] - fixed
        share_camera(it + 1)

        @pl.when(first)
        def _():
            @pl.when(group < n_g - 1)
            def _():
                ring_copy().wait_send()

            far_arrive(lambda source: group > source)
            pass_arrive(lambda source: group > source)

            @pl.when(inner_group)
            def _():
                far_each(lambda to: to >= 0, lambda copy: copy.wait_send())

        await_cameras(it + 1)
        return carry

    lax.fori_loop(0, ITERS, inner_step, 0)
    cam_out[...] = own[ITERS]
    cameras = every[ITERS].reshape(n_c * count, width)
    eliminate_points(
        False, cameras, pick, pick_t, cj_ref, pj_ref, res_ref,
        jnp.concatenate([high_damp] * 2, axis=1), point_out, seen, parts,
    )


def paired_shards(n_c, n_p, cam_jac, point_jac, residual, obs_cam, damp_exp, cam_step, diag_inverse, coupling):
    blocks, observers = obs_cam.shape
    count, width = cam_step.shape
    total_blocks = count * n_c
    pairs = observers // 2
    rows = pairs * blocks
    n_g = n_c // 2
    cj, pj, obs = cam_jac.transpose(1, 0, 2), point_jac.transpose(1, 0, 2), obs_cam.T
    res = residual.reshape(blocks, 2, pairs, 128).transpose(0, 2, 1, 3).reshape(2 * rows, 128)
    sem = pltpu.SemaphoreType.DMA

    def vmem(*shape, dtype=F32):
        return pltpu.VMEM(shape, dtype)

    camera, out = pl.pallas_call(
        functools.partial(paired_kernel, n_c, n_p),
        in_specs=[ANY] * 8,
        out_specs=[VMEM, VMEM],
        out_shape=[
            jax.ShapeDtypeStruct((count, width), F32),
            jax.ShapeDtypeStruct((3, blocks, 64), F32),
        ],
        scratch_shapes=[pltpu.VMEM(x.shape, x.dtype) for x in (obs, damp_exp, cj, pj, res, diag_inverse, coupling)]
        + [
            vmem(count, width // 2, width),
            vmem(count, 2, width, width),
            vmem(2, width, width),
            vmem(2, width, width),
            vmem(n_g - 2, width, width),
            vmem(width // 2, width),
            vmem(width, width),
            vmem(2 * rows, 3 * total_blocks, dtype=BF16),
            vmem(total_blocks, 2 * rows, dtype=BF16),
            vmem(2 * rows, width),
            vmem(2, 2 * rows, width, dtype=BF16),
            vmem(total_blocks, width),
            vmem(ITERS + 1, count, width),
            vmem(ITERS + 1, n_c, count, width),
            vmem(ITERS, n_c, count, width),
            vmem(ITERS, n_p, count, width),
            vmem(ITERS, n_p, 8, width),
            vmem(ITERS, n_p, 8, width),
            vmem(count, width),
            vmem(count, width),
            vmem(n_g, 8, width),
            vmem(ITERS, n_g, 8, width),
            vmem(8, width),
            vmem(8, width),
            vmem(8, width),
            sem((6,)), sem((2, count // 2)), sem((ITERS + 1,)), sem((ITERS + 1,)),
            sem((ITERS,)), sem((ITERS,)), sem((ITERS,)), sem((ITERS,)), sem((ITERS,)), sem((ITERS,)),
            sem((ITERS,)), sem((ITERS,)), sem(()), sem(()), sem((ITERS,)), sem((ITERS,)), sem(()), sem(()),
            sem((2,)), sem((2,)), sem((4,)), sem((4,)),
            sem((n_g,)), sem((n_g - 2,)), sem((n_g - 2,)), sem((n_g - 2,)), sem(()), sem(()),
        ],
        compiler_params=pltpu.CompilerParams(
            collective_id=0, has_side_effects=True, vmem_limit_bytes=60 << 20
        ),
        name="camera_steps",
    )(obs, damp_exp, cam_step, cj, pj, res, diag_inverse, coupling)
    return camera, out.transpose(1, 0, 2)


def solution(mesh):
    in_specs = (
        P(("chain", "pts"), None, None),
        P(("chain", "pts"), None, None),
        P(("chain", "pts"), None, None),
        P(("chain", "pts"), None),
        P(),
        P("chain", None),
        P("chain", None, None),
        P("chain", None, None),
    )
    out_specs = (P("chain", None), P(("chain", "pts"), None, None))
    n_c, n_p = mesh.shape["chain"], mesh.shape["pts"]
    paired = n_c in (8, 16) and n_p % 2 == 0
    inner = functools.partial(paired_shards if paired else shards, n_c, n_p)
    return jax.shard_map(inner, mesh=mesh, in_specs=in_specs, out_specs=out_specs, check_vma=False)
```
